256 devices in a mesh: ctx: 8 (over x, core), head: 4 (over y), exp: 8 (over z).
Axes of the slice: x: 4, y: 4, z: 8, core: 2. Of those that a mesh axis runs over, the one named last changes fastest.
Arguments:
- resid: bfloat16 [8192, 2048], P(('ctx', 'exp')), may hold values from -6 to 6
- queries: bfloat16 [8192, 4096], P(('ctx', 'exp'), 'head'), may hold values from -42 to 42
- rotated_key_value_pairs: bfloat16 [2, 8192, 512], P(None, ('ctx', 'exp'), 'head'), may hold values from -13 to 13
- doc_ids: int32 [1, 8192], P(None, ('ctx', 'exp')), may hold values from 0 to 5, never falling along the last dimension, each value on 1 to 6144 neighbouring positions
- out_weight: bfloat16 [4096, 2048], P('head', ('ctx', 'exp')), may hold values from -0.09375 to 0.09375
- norm_gain: float32 [2048], replicated, may hold values from 0.1 to 1.9
- routes: int32 [8192, 8], P(('ctx', 'exp')), may hold values from 0 to 127, all different within a row; in each aligned block of 128 rows (0 to 127, 128 to 255, ...) at most 10 rows name the same one
- probs: float32 [8192, 8], P(('ctx', 'exp')), may hold values from 0.05 to 0.3
- w_gate: bfloat16 [128, 768, 2048], P(('ctx', 'exp'), None, 'head'), may hold values from -0.125 to 0.125
- w_up: bfloat16 [128, 768, 2048], P(('ctx', 'exp'), None, 'head'), may hold values from -0.125 to 0.125
- w_down: bfloat16 [128, 768, 2048], P(('ctx', 'exp'), None, 'head'), may hold values from -0.21875 to 0.21875
- cotangent: bfloat16 [8192, 2048], P(('ctx', 'exp')), may hold values from -6 to 6
Outputs:
- layer_out: bfloat16 [8192, 2048], P(('ctx', 'exp'), 'head')
- grad_gate: bfloat16 [128, 768, 2048], P(('ctx', 'exp'), None, 'head')
- grad_up: bfloat16 [128, 768, 2048], P(('ctx', 'exp'), None, 'head')
- grad_down: bfloat16 [128, 768, 2048], P(('ctx', 'exp'), None, 'head')
The draws below stay inside these ranges and needn't reach their ends.
Inputs may be any that keep to these rules, and one draw needn't show every extreme that they name: `routes`: in the rows of one index of ctx+exp (aligned blocks of 128 rows) no expert is named more than 10 times, a bound that some block reaches; a row names 8 different experts. `doc_ids`: ids never fall along positions; a document spans 1 to 6144 positions, one exactly 6144.
All inputs are finite; a program needn't handle non-finite values.
Results may differ from the reference program's by a relative error of at most 0.018.
Values may be sent and summed in bfloat16 or wider, within the bound.
No kernel may reach another device: no remote copies, remote signals or barrier semaphores. Data moves between devices by JAX's collectives and lax.ppermute only.
A program may use at most 128 MiB of HBM per device.

```python
import math
import jax
import jax.numpy as jnp
import numpy as np
from jax import lax

D = 2048
QUERY_HEADS = 32
KEY_VALUE_HEADS = 4
HEAD_DIMENSION = 128
FF = 768
TOPK = 8
TOK_DEV = 128
DOCS = 6
EXPERTS = 128
WINDOW_TOKENS = 8192
CAP = 10
DOC_MOST = 6144


def drawn_pair(key):
    key_unrotated = jnp.clip(jax.random.normal(jax.random.fold_in(key, 11), (WINDOW_TOKENS, KEY_VALUE_HEADS, HEAD_DIMENSION), jnp.float32), -4.0, 4.0)
    value_unprojected = jnp.clip(jax.random.normal(jax.random.fold_in(key, 12), (WINDOW_TOKENS, KEY_VALUE_HEADS * HEAD_DIMENSION), jnp.float32), -4.0, 4.0)
    query_noise = jnp.clip(jax.random.normal(jax.random.fold_in(key, 13), (WINDOW_TOKENS, QUERY_HEADS * HEAD_DIMENSION), jnp.float32), -4.0, 4.0)
    group_width = QUERY_HEADS // KEY_VALUE_HEADS
    half_window = WINDOW_TOKENS // 2
    earlier_keys = jnp.roll(key_unrotated, half_window, axis=0)
    later_half = (jnp.arange(WINDOW_TOKENS, dtype=jnp.int32) >= half_window).astype(jnp.float32)
    earlier_wide = jnp.broadcast_to(earlier_keys[:, :, None, :], (WINDOW_TOKENS, KEY_VALUE_HEADS, group_width, HEAD_DIMENSION)).reshape(WINDOW_TOKENS, QUERY_HEADS * HEAD_DIMENSION)
    query_raw = query_noise + 0.9 * later_half[:, None] * earlier_wide
    key_rotated_final = key_unrotated
    query_final = query_raw
    stacked_pairs = jnp.stack([key_rotated_final.reshape(WINDOW_TOKENS, KEY_VALUE_HEADS * HEAD_DIMENSION), value_unprojected], axis=0)
    return (query_final, stacked_pairs)


def draw_queries(key, part):
    return drawn_pair(key)[0].astype(jnp.bfloat16)


def draw_rotated_key_value_pairs(key, part):
    return drawn_pair(key)[1].astype(jnp.bfloat16)


def levels(key, dims, split, low, top_value):
    def one(axis_at, parts):
        draws = jax.random.uniform(jax.random.fold_in(jax.random.fold_in(key, 6), axis_at), (parts,), jnp.float32, low / len(split), top_value / len(split))
        return jnp.repeat(jnp.exp(draws), dims[axis_at] // parts).reshape((-1,) + (1,) * (len(dims) - axis_at - 1))

    level = one(*split[0])
    for cut in split[1:]:
        level = level * one(*cut)
    return level


def length_profile(number_of, total, most, skew):
    portions = [(1 << 20) // math.isqrt(standing ** skew) + 1 for standing in range(2, number_of + 1)]
    spare, holding = total - most - (number_of - 1), [1] * (number_of - 1)
    while spare > 0:
        free = [i for i in range(number_of - 1) if holding[i] < most]
        pool, left = sum([portions[i] for i in free]), spare
        for i in free:
            more = min(most - holding[i], max(1, left * portions[i] // pool), spare)
            holding[i] = holding[i] + more
            spare = spare - more
    return np.array([most] + holding)


def ragged(key, amount, total, reach, slope):
    if amount == 2:
        one = jax.random.randint(key, (), max(1, total - reach), min(reach, total - 1) + 1)
        return jnp.stack([one, total - one])
    lengths = jnp.asarray(length_profile(amount, total, reach, slope), jnp.int32)
    twos = (amount - 1) // 2
    donor, sink = lengths[1:1 + 2 * twos:2], lengths[2:2 + 2 * twos:2]
    slack = jnp.minimum(donor - 1, reach - sink)
    shifted = jax.random.randint(jax.random.fold_in(key, 1), (twos,), 0, 1 << 20) % (slack + 1)
    lengths = lengths.at[1:1 + 2 * twos:2].set(donor - shifted).at[2:2 + 2 * twos:2].set(sink + shifted)
    return lengths[jax.random.permutation(jax.random.fold_in(key, 2), amount)]


def assign_block(key, own, number, rows, count, top, limit, lean):
    order = jax.random.permutation(key, count)
    packed, ordinary = load_shares(count, rows * top, limit, lean, True), load_shares(count, rows * top, limit, lean, False)
    places = jnp.arange(count)

    def named(sizes, turn):
        used = int((sizes > 0).sum())
        fixed = max(1, used // 4)
        shifted = fixed + (places - fixed + turn * (used - fixed)) % max(1, count - fixed)
        return jnp.zeros((count,), jnp.int32).at[order[jnp.where(places < fixed, places, shifted)]].set(jnp.asarray(sizes, jnp.int32))

    sizes = jnp.where(number % 4 == 0, named(packed, number // 4), named(ordinary, number - number // 4 - 1))
    mixed = jax.random.permutation(jax.random.fold_in(own, 3), count)
    giver, sink = mixed[0:count // 2 * 2:2], mixed[1:count // 2 * 2:2]
    room = jnp.minimum(sizes[giver] - 1, limit - sizes[sink]) // 2
    room = jnp.where((giver == order[0]) | (sink == order[0]) | (sizes[sink] == 0), 0, jnp.maximum(room, 0))
    shifted = jax.random.randint(jax.random.fold_in(own, 4), (count // 2,), 0, 1 << 20) % (room + 1)
    sizes = sizes.at[giver].add(-shifted).at[sink].add(shifted)
    members = jnp.searchsorted(jnp.cumsum(sizes), jnp.arange(rows * top), side="right").astype(jnp.int32)
    listing = members.reshape(top, rows).T
    listing = listing[jax.random.permutation(jax.random.fold_in(own, 1), rows)]
    turn = jax.random.randint(jax.random.fold_in(own, 2), (rows, 1), 0, top)
    return jnp.take_along_axis(listing, (jnp.arange(top)[None, :] + turn) % top, axis=1)


def load_shares(number_of, total, limit, slope, full):
    loads = [(1 << 20) // math.isqrt(standing ** slope) + 1 for standing in range(1, number_of + 1)]
    largest = limit if full else min(limit, max(-(-total // number_of), total * loads[0] // sum(loads)))
    least = 1 if total - largest >= number_of - 1 else 0
    counts, surplus = [largest] + [least] * (number_of - 1), total - largest - least * (number_of - 1)
    while surplus > 0:
        candidates = [i for i in range(1, number_of) if counts[i] < largest] or [i for i in range(1, number_of) if counts[i] < limit]
        mass, remaining = sum([loads[i] for i in candidates]), surplus
        for i in candidates:
            more = min(limit - counts[i], max(1, remaining * loads[i] // mass), surplus)
            counts[i] = counts[i] + more
            surplus = surplus - more
    return np.array(counts)


def noise(own_key, extent, width, bound, split=(), held_as=jnp.bfloat16):
    drawn = width * jax.random.normal(own_key, extent, jnp.float32)
    if split:
        drawn = drawn * levels(own_key, extent, split, -0.22, 0.18)
    return jnp.clip(drawn, -bound, bound).astype(held_as)


def setup_inputs(seed: int = 0) -> dict:
    key_of = jax.random.split(jax.random.key(seed), 13)
    resid = noise(key_of[0], (WINDOW_TOKENS, D), 1.0, 6.0, ((0, 64),))
    queries = draw_queries(jax.random.fold_in(key_of[12], 71), 0)
    rotated_key_value_pairs = draw_rotated_key_value_pairs(jax.random.fold_in(key_of[12], 71), 0)
    doc_ids = jax.vmap(lambda own: jnp.searchsorted(jnp.cumsum(ragged(own, DOCS, WINDOW_TOKENS, DOC_MOST, 1)), jnp.arange(WINDOW_TOKENS), side="right"))(jax.random.split(key_of[3], 1)).reshape((1, WINDOW_TOKENS)).astype(jnp.int32)
    out_weight = noise(key_of[4], (QUERY_HEADS * HEAD_DIMENSION, D), (QUERY_HEADS * HEAD_DIMENSION) ** -0.5, 0.09375, ((0, 4), (1, 64)))
    norm_gain = jnp.clip(1.0 + 0.18 * jax.random.normal(key_of[5], (D,), jnp.float32), 0.1, 1.9)
    routes_keys = jax.random.split(jax.random.fold_in(key_of[6], 1), WINDOW_TOKENS // TOK_DEV)
    routes_turns = jax.random.permutation(jax.random.fold_in(key_of[6], 3), WINDOW_TOKENS // TOK_DEV)
    routes = jax.vmap(lambda own, number: assign_block(jax.random.fold_in(key_of[6], 2), own, number, TOK_DEV, EXPERTS, TOPK, CAP, 2))(routes_keys, routes_turns).reshape((WINDOW_TOKENS, TOPK))
    probs = jnp.clip(0.05 + 0.25 * jax.random.uniform(key_of[7], (WINDOW_TOKENS, TOPK), jnp.float32) ** levels(key_of[7], (WINDOW_TOKENS, TOPK), ((0, 64),), -0.2, 0.2), 0.05, 0.3)
    w_gate = noise(key_of[8], (EXPERTS, FF, D), D ** -0.5, 0.125, ((0, 64), (2, 4)))
    w_up = noise(key_of[9], (EXPERTS, FF, D), D ** -0.5, 0.125, ((0, 64), (2, 4)))
    w_down = noise(key_of[10], (EXPERTS, FF, D), FF ** -0.5, 0.21875, ((0, 64), (2, 4)))
    cotangent = noise(key_of[11], (WINDOW_TOKENS, D), 1.0, 6.0, ((0, 64),))
    return dict(resid=resid, queries=queries, rotated_key_value_pairs=rotated_key_value_pairs, doc_ids=doc_ids, out_weight=out_weight, norm_gain=norm_gain, routes=routes, probs=probs, w_gate=w_gate, w_up=w_up, w_down=w_down, cotangent=cotangent)


def reference(resid, queries, rotated_key_value_pairs, doc_ids, out_weight, norm_gain, routes, probs, w_gate, w_up, w_down, cotangent):
    group_width = QUERY_HEADS // KEY_VALUE_HEADS
    q_heads = queries.reshape(WINDOW_TOKENS, QUERY_HEADS, HEAD_DIMENSION)
    key_head_count = rotated_key_value_pairs[0].reshape(WINDOW_TOKENS, KEY_VALUE_HEADS, HEAD_DIMENSION)
    value_head_count = rotated_key_value_pairs[1].reshape(WINDOW_TOKENS, KEY_VALUE_HEADS, HEAD_DIMENSION)
    doc_row = doc_ids[0]
    positions = jnp.arange(WINDOW_TOKENS, dtype=jnp.int32)
    block_rows = min(512, WINDOW_TOKENS)
    block_count = WINDOW_TOKENS // block_rows
    score_scale = HEAD_DIMENSION ** (-0.5)

    def one_head(head_id):
        queries_h = jnp.take(q_heads, head_id, axis=1)
        keys_h = jnp.take(key_head_count, head_id // group_width, axis=1)
        values_h = jnp.take(value_head_count, head_id // group_width, axis=1)

        def one_block(block_id):
            first_row = block_id * block_rows
            query_rows = lax.dynamic_slice_in_dim(queries_h, first_row, block_rows, 0)
            query_pos = first_row + jnp.arange(block_rows, dtype=jnp.int32)
            query_doc = lax.dynamic_slice_in_dim(doc_row, first_row, block_rows, 0)
            scores = jnp.dot(query_rows, keys_h.T, preferred_element_type=jnp.float32) * score_scale
            visible = (positions[None, :] <= query_pos[:, None]) & (doc_row[None, :] == query_doc[:, None])
            scores = jnp.where(visible, scores, -1e+30)
            row_max = lax.optimization_barrier(jnp.max(scores, axis=-1, keepdims=True))
            weights = jnp.where(visible, jnp.exp(scores - row_max), 0.0)
            row_total = lax.optimization_barrier(jnp.sum(weights, axis=-1))
            mixed = jnp.dot(weights.astype(jnp.bfloat16), values_h, preferred_element_type=jnp.float32)
            return (mixed / row_total[:, None]).astype(jnp.bfloat16)
        return lax.map(one_block, jnp.arange(block_count, dtype=jnp.int32)).reshape(WINDOW_TOKENS, HEAD_DIMENSION)
    attn = lax.map(one_head, jnp.arange(QUERY_HEADS, dtype=jnp.int32))
    attn = jnp.transpose(attn, (1, 0, 2)).reshape(WINDOW_TOKENS, QUERY_HEADS * HEAD_DIMENSION)
    projected = jnp.dot(attn, out_weight, preferred_element_type=jnp.float32)
    hidden_state = (resid.astype(jnp.float32) + projected).astype(jnp.bfloat16)
    hstate = hidden_state.astype(jnp.float32)
    inverse = lax.rsqrt(lax.optimization_barrier(jnp.mean(hstate * hstate, axis=-1, keepdims=True)) + 1e-06)
    normed = (hstate * inverse * norm_gain).astype(jnp.bfloat16)
    flat_routes = routes.reshape(-1)
    assigned = WINDOW_TOKENS * TOPK
    per_block = TOK_DEV * TOPK
    block_total = WINDOW_TOKENS // TOK_DEV
    onehot = (flat_routes.reshape(block_total, per_block, 1) == jnp.arange(EXPERTS, dtype=jnp.int32)[None, None, :]).astype(jnp.int32)
    slot_rank = lax.optimization_barrier(jnp.sum((jnp.cumsum(onehot, axis=1) - onehot) * onehot, axis=2)).reshape(-1)
    block_of = jnp.arange(assigned, dtype=jnp.int32) // per_block
    slot_index = (flat_routes * block_total + block_of) * CAP + slot_rank
    slot_owner = jnp.full((EXPERTS * block_total * CAP,), assigned, jnp.int32)
    slot_owner = slot_owner.at[slot_index].set(jnp.arange(assigned, dtype=jnp.int32))
    slot_owner = slot_owner.reshape(EXPERTS, block_total * CAP)
    normed_pad = jnp.concatenate([normed, jnp.zeros((1, D), jnp.bfloat16)], axis=0)
    cot_pad = jnp.concatenate([cotangent, jnp.zeros((1, D), jnp.bfloat16)], axis=0)
    probs_pad = jnp.concatenate([probs.reshape(-1), jnp.zeros((1,), jnp.float32)])

    def one_expert(accum, inputs):
        owner_rows, gate_w, up_w, down_w = inputs
        token_rows = owner_rows // TOPK
        slot_inputs = normed_pad[token_rows]
        slot_probs = probs_pad[owner_rows]
        slot_grads = (slot_probs[:, None] * cot_pad[token_rows].astype(jnp.float32)).astype(jnp.bfloat16)
        gate_act = jnp.dot(slot_inputs, gate_w.T, preferred_element_type=jnp.float32)
        up_act = jnp.dot(slot_inputs, up_w.T, preferred_element_type=jnp.float32)
        sigma = jax.nn.sigmoid(gate_act)
        silu_gate = gate_act * sigma
        hidden = (silu_gate * up_act).astype(jnp.bfloat16)
        rounded_out = lax.optimization_barrier(jnp.dot(hidden, down_w, preferred_element_type=jnp.float32).astype(jnp.bfloat16))
        expert_out = rounded_out.astype(jnp.float32)
        accum = accum.at[token_rows].add(slot_probs[:, None] * expert_out, mode='drop')
        hidden_grad = jnp.dot(slot_grads, down_w.T, preferred_element_type=jnp.float32)
        gate_grad = (hidden_grad * up_act * sigma * (1.0 + gate_act * (1.0 - sigma))).astype(jnp.bfloat16)
        up_grad = (hidden_grad * silu_gate).astype(jnp.bfloat16)
        down_out = jnp.dot(hidden.T, slot_grads, preferred_element_type=jnp.float32).astype(jnp.bfloat16)
        gate_out = jnp.dot(gate_grad.T, slot_inputs, preferred_element_type=jnp.float32).astype(jnp.bfloat16)
        up_out = jnp.dot(up_grad.T, slot_inputs, preferred_element_type=jnp.float32).astype(jnp.bfloat16)
        return (accum, (gate_out, up_out, down_out))
    accum, grads = lax.scan(one_expert, jnp.zeros((WINDOW_TOKENS, D), jnp.float32), (slot_owner, w_gate, w_up, w_down))
    layer_out = (hstate + accum).astype(jnp.bfloat16)
    return (layer_out, grads[0], grads[1], grads[2])
```

```python
import functools
import math

import jax
import jax.numpy as jnp
from jax import lax
from jax.experimental import pallas as pl
from jax.experimental.pallas import tpu as pltpu
from jax.sharding import PartitionSpec as P

BF = jnp.bfloat16
F32 = jnp.float32
HD = 128
CAP = 10
ROW = 24
RELZ = (-1, 0, 1, -4, -3, -2, 2, 3)
NT = (((1,), (1,)), ((), ()))
TN = (((0,), (0,)), ((), ()))
ANY = pl.BlockSpec(memory_space=pl.ANY)
VM = pl.BlockSpec(memory_space=pltpu.VMEM)


def shift(x, axis, n, d):
    return lax.ppermute(x, axis, [(i, (i + d) % n) for i in range(n)])


def shift_x(x, d):
    return lax.ppermute(x, "ctx", [(i, (i + 2 * d) % 8) for i in range(8)])


def swap_core(x):
    return lax.ppermute(x, "ctx", [(i, i ^ 1) for i in range(8)])


def gather_z(x, axis0_rows):
    n = axis0_rows
    before, after = shift(x, "exp", 8, 1), shift(x, "exp", 8, -1)
    three = jnp.concatenate([before, x, after], 0)
    far_before = shift(three, "exp", 8, 3)
    far_after = shift(three[: 2 * n], "exp", 8, -3)
    return jnp.concatenate([three, far_before, far_after], 0)


def attention_kernel(q_ref, qdoc_ref, *refs):
    pieces = refs[:10]
    o_ref, kv, qs, bias, m_s, l_s, acc, sem = refs[10:]
    plan = ((0, 0, 8), (1, 0, 8), (2, 0, 8), (3, 0, 4), (3, 4, 4))
    copies = []
    for core in range(2):
        for p, (c, lo, n) in enumerate(plan):
            k = core * 5 + p
            copies.append(
                pltpu.make_async_copy(
                    pieces[k], kv.at[core * 4 + c, pl.ds(lo, n)], sem.at[k]
                )
            )
    for cp in copies:
        cp.start()
    ctx = lax.axis_index("ctx")
    z = lax.axis_index("exp")
    me = ctx * 8 + z
    for h in range(8):
        qs[h * 128 : (h + 1) * 128, :] = q_ref[:, h * 128 : (h + 1) * 128]
    m_s[...] = jnp.full(m_s.shape, -1e30, F32)
    l_s[...] = jnp.zeros(l_s.shape, F32)
    acc[...] = jnp.zeros(acc.shape, F32)
    qdoc = qdoc_ref[...].astype(F32)
    first_doc = jnp.min(qdoc)
    row = lax.broadcasted_iota(jnp.int32, (128, 128), 0)
    lane = lax.broadcasted_iota(jnp.int32, (128, 128), 1)
    coef = HD**-0.5 * math.log2(math.e)
    for cp in copies:
        cp.wait()

    def chunk(c, carry):
        core = c // 4
        k = c % 4
        dx = jnp.where(k == 1, 3, jnp.where(k == 2, 1, jnp.where(k == 3, 2, 0)))
        own_core = ctx % 2
        kcore = jnp.where(core == 0, own_core, 1 - own_core)
        kctx = ((ctx // 2 + dx) % 4) * 2 + kcore
        docs = kv[c, :, 256:272, :].astype(F32)
        last_doc = jnp.max(docs)

        @pl.when((kctx <= ctx) & (last_doc >= first_doc))
        def _():
            for b, rel in enumerate(RELZ):
                j = kctx * 8 + (z + rel + 8) % 8
                seen = (lane + j * 128 <= row + me * 128) & (
                    docs[b, 0:1, :] == qdoc
                )
                bias[:, b * 128 : (b + 1) * 128] = jnp.where(seen, 0.0, -1e30)

            def group(g, carry2):
                r = pl.ds(pl.multiple_of(g * 256, 256), 256)
                keys = kv[c, :, 0:128, :].reshape(1024, 128)
                vals = kv[c, :, 128:256, :].reshape(1024, 128)
                s = lax.dot_general(qs[r, :], keys, NT, preferred_element_type=F32)
                s = s * coef
                s = (s.reshape(2, 128, 1024) + bias[...][None]).reshape(256, 1024)
                old = m_s[r, :]
                new = jnp.maximum(old, jnp.max(s, axis=1, keepdims=True))
                keep = jnp.exp2(old - new)
                p = jnp.exp2(s - new[:, 0:1])
                part = p[:, 0:128]
                for i in range(1, 8):
                    part = part + p[:, i * 128 : (i + 1) * 128]
                l_s[r, :] = l_s[r, :] * keep + part
                m_s[r, :] = new
                acc[r, :] = acc[r, :] * keep + lax.dot_general(
                    p.astype(BF), vals, (((1,), (0,)), ((), ())), preferred_element_type=F32
                )
                return carry2

            lax.fori_loop(0, 4, group, 0)

        return carry

    lax.fori_loop(0, 8, chunk, 0)
    for h in range(8):
        r = slice(h * 128, (h + 1) * 128)
        total = jnp.sum(l_s[r, :], axis=1, keepdims=True)
        o_ref[:, r] = (acc[r, :] / total).astype(BF)


def attention(queries, doc_col, pieces):
    return pl.pallas_call(
        attention_kernel,
        out_shape=jax.ShapeDtypeStruct((128, 1024), BF),
        in_specs=[VM, VM] + [ANY] * 10,
        out_specs=VM,
        scratch_shapes=[
            pltpu.VMEM((8, 8, 272, 128), BF),
            pltpu.VMEM((1024, 128), BF),
            pltpu.VMEM((128, 1024), F32),
            pltpu.VMEM((1024, 128), F32),
            pltpu.VMEM((1024, 128), F32),
            pltpu.VMEM((1024, 128), F32),
            pltpu.SemaphoreType.DMA((10,)),
        ],
        name="attention",
    )(queries, doc_col, *pieces)


def project_kernel(attn_ref, wa_ref, wb_ref, o0, o1, o2, o3, ws):
    ctx = lax.axis_index("ctx")
    z = lax.axis_index("exp")
    me = lax.axis_index("head")
    own = ctx % 2
    for k, ref in enumerate((wa_ref, wb_ref)):
        core = own if k == 0 else 1 - own
        for zi, rel in enumerate(RELZ):
            for xi, dx in enumerate((0, 3, 1, 2)):
                at = ((ctx // 2 + dx) % 4) * 512 + core * 256 + ((z + rel + 8) % 8) * 32
                src = zi * 128 + xi * 32
                ws[pl.ds(pl.multiple_of(at, 32), 32), :] = ref[src : src + 32, :]
    for d, out in enumerate((o0, o1, o2, o3)):
        at = pl.multiple_of(((me + d) % 4) * 512, 512)
        part = lax.dot_general(
            attn_ref[...], ws[pl.ds(at, 512), :], NT, preferred_element_type=F32
        )
        out[...] = part.astype(out.dtype)


def project(attn, wa, wb):
    return pl.pallas_call(
        project_kernel,
        out_shape=[jax.ShapeDtypeStruct((128, 512), F32)]
        + [jax.ShapeDtypeStruct((128, 512), BF)] * 3,
        in_specs=[VM] * 3,
        out_specs=[VM] * 4,
        scratch_shapes=[pltpu.VMEM((2048, 1024), BF)],
        name="project",
    )(attn, wa, wb)


def route_kernel(routes_ref, probs_ref, cot_ref, pick_ref, grad_ref, hi_ref, lo_ref):
    expert = lax.broadcasted_iota(jnp.int32, (128, 128), 0)
    named = jnp.zeros((128, 128), F32)
    weight = jnp.zeros((128, 128), F32)
    for k in range(8):
        hit = routes_ref[k : k + 1, :] == expert
        named = named + jnp.where(hit, 1.0, 0.0)
        weight = weight + jnp.where(hit, probs_ref[k : k + 1, :], 0.0)
    earlier = (
        lax.broadcasted_iota(jnp.int32, (128, 128), 0)
        < lax.broadcasted_iota(jnp.int32, (128, 128), 1)
    )
    rank = jnp.dot(
        named.astype(BF),
        jnp.where(earlier, 1.0, 0.0).astype(BF),
        preferred_element_type=F32,
    )
    place = (named * (rank + 1.0)).astype(BF)
    w1 = weight.astype(BF)
    rest = weight - w1.astype(F32)
    w2 = rest.astype(BF)
    w3 = (rest - w2.astype(F32)).astype(BF)
    size = 384
    for part in range(4):
        r = lax.broadcasted_iota(jnp.int32, (size, 128), 0)
        owner = jnp.zeros((size, 128), jnp.int32)
        for o in range(1, 16):
            owner = owner + jnp.where(r >= o * ROW, 1, 0)
        inner = r - owner * ROW
        second = jnp.where(inner >= CAP, 1, 0)
        slot = inner - second * CAP
        slot = jnp.where(inner >= 2 * CAP, 1000, slot)
        of = (owner + part * 16) * 2 + second
        chosen = jnp.where(
            of == lax.broadcasted_iota(jnp.int32, (size, 128), 1), 1.0, 0.0
        ).astype(BF)
        dot = functools.partial(jnp.dot, preferred_element_type=F32)
        mine = dot(chosen, place) == (slot + 1).astype(F32)
        w = (dot(chosen, w1) + dot(chosen, w2)) + dot(chosen, w3)
        w = jnp.where(mine, w, 0.0)
        pick = jnp.where(mine, 1.0, 0.0).astype(BF)
        at = slice(part * size, (part + 1) * size)
        pick_ref[at, :] = pick
        scale = jnp.sum(w, axis=1, keepdims=True)
        grad_ref[at, :] = (scale * dot(pick, cot_ref[...])).astype(BF)
        hi = w.astype(BF)
        hi_ref[at, :] = hi
        lo_ref[at, :] = (w - hi.astype(F32)).astype(BF)


def route(routes_t, probs_t, cot):
    rows = 64 * ROW
    sq = jax.ShapeDtypeStruct((rows, 128), BF)
    return pl.pallas_call(
        route_kernel,
        out_shape=[sq, jax.ShapeDtypeStruct((rows, 512), BF), sq, sq],
        in_specs=[VM] * 3,
        out_specs=[VM] * 4,
        name="route",
    )(routes_t, probs_t, cot)


def share_kernel(xa_ref, wa_ref, xb_ref, wb_ref, own, up, down, keep1, keep3, s):
    me = lax.axis_index("head")
    s[:, 0:768] = lax.dot_general(xa_ref[...], wa_ref[...], NT, preferred_element_type=F32)
    s[:, 768:1536] = lax.dot_general(
        xb_ref[...], wb_ref[...], NT, preferred_element_type=F32
    )

    def rows(d, lo, n):
        at = pl.multiple_of(((me + d) % 4) * 160 + lo, 16)
        return s[pl.ds(at, n), :]

    own[...] = rows(0, 0, 160)
    up[0:80, :] = rows(2, 0, 80).astype(BF)
    up[80:160, :] = rows(1, 80, 80).astype(BF)
    down[0:80, :] = rows(2, 80, 80).astype(BF)
    down[80:160, :] = rows(3, 0, 80).astype(BF)
    keep1[...] = rows(1, 0, 80)
    keep3[...] = rows(3, 80, 80)


def share(xa, wa, ia, xb, wb, ib):
    def weight(i):
        return pl.BlockSpec((None, 768, 512), lambda g: (i, 0, 0))

    def whole(shape):
        return pl.BlockSpec(shape, lambda g: (0, 0))

    shapes = [((160, 1536), F32), ((160, 1536), BF), ((160, 1536), BF)]
    shapes += [((80, 1536), F32), ((80, 1536), F32)]
    return pl.pallas_call(
        share_kernel,
        out_shape=[jax.ShapeDtypeStruct(a, b) for a, b in shapes],
        grid=(1,),
        in_specs=[whole((640, 512)), weight(ia), whole((640, 512)), weight(ib)],
        out_specs=[whole(a) for a, b in shapes],
        scratch_shapes=[pltpu.VMEM((640, 1536), F32)],
        name="share",
    )(xa, wa, xb, wb)


def add_head(parts):
    own, up, down, keep1, keep3 = parts
    below, above = shift(up, "head", 4, 1), shift(down, "head", 4, -1)
    relay1 = (keep1 + below[:80].astype(F32)).astype(BF)
    relay3 = (keep3 + above[:80].astype(F32)).astype(BF)
    far1, far3 = shift(relay1, "head", 4, 1), shift(relay3, "head", 4, -1)
    return own, below, above, far1, far3


def total(own, below, above, far1, far3, cols):
    lo = (own[0:80, cols] + above[80:160, cols].astype(F32)) + far1[:, cols].astype(F32)
    hi = (own[80:160, cols] + below[80:160, cols].astype(F32)) + far3[:, cols].astype(F32)
    return lo, hi


def hidden_kernel(own, below, above, far1, far3, out):
    gates = total(own, below, above, far1, far3, slice(0, 768))
    ups = total(own, below, above, far1, far3, slice(768, 1536))
    for i in range(2):
        sigma = 1.0 / (1.0 + jnp.exp(-gates[i]))
        out[i * 80 : (i + 1) * 80, :] = (gates[i] * sigma * ups[i]).astype(BF)


def hidden_share(arrived):
    return pl.pallas_call(
        hidden_kernel,
        out_shape=jax.ShapeDtypeStruct((160, 768), BF),
        in_specs=[VM] * 5,
        out_specs=VM,
        name="hidden",
    )(*arrived)


def grads_kernel(*refs):
    acts, grad, out = (refs[0:5], refs[5:10]), refs[10:15], refs[15]
    for e in range(2):
        gates = total(*acts[e], slice(0, 768))
        ups = total(*acts[e], slice(768, 1536))
        back = total(*grad, slice(e * 768, (e + 1) * 768))
        for i in range(2):
            r = slice(i * 80, (i + 1) * 80)
            sigma = 1.0 / (1.0 + jnp.exp(-gates[i]))
            gg = back[i] * ups[i] * sigma * (1.0 + gates[i] * (1.0 - sigma))
            out[r, e * 1536 : e * 1536 + 768] = gg.astype(BF)
            out[r, e * 1536 + 768 : (e + 1) * 1536] = (back[i] * (gates[i] * sigma)).astype(BF)


def grads_share(act0, act1, grad):
    return pl.pallas_call(
        grads_kernel,
        out_shape=jax.ShapeDtypeStruct((160, 3072), BF),
        in_specs=[VM] * 15,
        out_specs=VM,
        name="grads",
    )(*act0, *act1, *grad)


def gather_head(x):
    below, above = shift(x, "head", 4, 1), shift(x, "head", 4, -1)
    far_a, far_b = shift(below[:80], "head", 4, 1), shift(above[80:], "head", 4, -1)
    return x, below, above, far_a, far_b


def assemble(me, refs, out, cols):
    x, below, above, far_a, far_b = refs
    for d, lo, n, ref in (
        (0, 0, 160, x),
        (3, 0, 160, below),
        (1, 0, 160, above),
        (2, 0, 80, far_a),
        (2, 80, 80, far_b),
    ):
        at = pl.multiple_of(((me + d) % 4) * 160 + lo, 16)
        out[pl.ds(at, n), :] = ref[:, cols]


def down_kernel(x, below, above, far_a, far_b, w_ref, out, h):
    me = lax.axis_index("head")
    assemble(me, (x, below, above, far_a, far_b), h, slice(0, 768))
    out[...] = jnp.dot(h[...], w_ref[...], preferred_element_type=F32).astype(BF)


def down(hidden, w_down, e):
    def whole(shape):
        return pl.BlockSpec(shape, lambda g: (0, 0))

    return pl.pallas_call(
        down_kernel,
        out_shape=jax.ShapeDtypeStruct((640, 512), BF),
        grid=(1,),
        in_specs=[whole(a.shape) for a in hidden]
        + [pl.BlockSpec((None, 768, 512), lambda g: (e, 0, 0))],
        out_specs=whole((640, 512)),
        scratch_shapes=[pltpu.VMEM((640, 768), BF)],
        name="down",
    )(*hidden, w_down)


def weight_grad_kernel(n_out, *refs):
    me = lax.axis_index("head")
    pieces, right, outs, t = refs[:10], refs[10:12], refs[12 : 12 + n_out], refs[12 + n_out]
    for e in range(2):
        for k in range(n_out):
            if n_out == 1:
                assemble(me, pieces[e * 5 : e * 5 + 5], t, slice(0, 768))
            else:
                lo = e * 1536 + k * 768
                assemble(me, pieces[:5], t, slice(lo, lo + 768))
            outs[k][e] = lax.dot_general(
                t[...], right[e][...], TN, preferred_element_type=F32
            ).astype(BF)


def weight_grads(pieces, right, n_out):
    pieces = list(pieces)
    if len(pieces) == 5:
        pieces = pieces + [jnp.zeros((16, 128), BF)] * 5
    return pl.pallas_call(
        functools.partial(weight_grad_kernel, n_out),
        out_shape=[jax.ShapeDtypeStruct((2, 768, 512), BF)] * n_out,
        in_specs=[VM] * 12,
        out_specs=[VM] * n_out,
        scratch_shapes=[pltpu.VMEM((640, 768), BF)],
        name="weight_grads",
    )(*pieces, *right)


def spread(got):
    got = got.reshape(64, ROW, 512)
    return [got[:, e * CAP : (e + 1) * CAP].reshape(640, 512) for e in range(2)]


def exchange(x):
    return lax.all_to_all(
        x.reshape(64, ROW, 512), ("ctx", "exp"), split_axis=0, concat_axis=0, tiled=True
    )


def per_device(
    resid,
    queries,
    rotated_key_value_pairs,
    doc_ids,
    out_weight,
    norm_gain,
    routes,
    probs,
    w_gate,
    w_up,
    w_down,
    cotangent,
):
    head = lax.axis_index("head")
    packed = jnp.concatenate(
        [
            rotated_key_value_pairs.reshape(256, 128),
            jnp.broadcast_to(doc_ids.astype(BF), (16, 128)),
        ],
        0,
    )
    z0 = gather_z(packed, 272).reshape(8, 272, 128)
    below, above = shift_x(z0, 1), shift_x(z0, -1)
    far_a, far_b = shift_x(below[:4], 1), shift_x(above[4:], -1)
    own_pieces = (z0, below, above, far_a, far_b)
    pieces = own_pieces + tuple(swap_core(p) for p in own_pieces)
    wt = out_weight.T
    wx = jnp.concatenate([wt, shift_x(wt, 1), shift_x(wt, -1), shift_x(wt, 2)], 0)
    wa = gather_z(wx, 128)
    wb = swap_core(wa)

    attn = attention(queries, doc_ids.reshape(128, 1), pieces)
    o0, o1, o2, o3 = project(attn, wa, wb)
    attn_sum = (o0 + shift(o1, "head", 4, 1).astype(F32)) + (
        shift(o2, "head", 4, 2).astype(F32) + shift(o3, "head", 4, -1).astype(F32)
    )
    own_resid = lax.dynamic_slice_in_dim(resid, head * 512, 512, 1)
    hstate = (own_resid.astype(F32) + attn_sum).astype(BF).astype(F32)
    square = jnp.sum(hstate * hstate, axis=-1).reshape(1, 128)
    square = (square + shift(square, "head", 4, 1)) + (
        shift(square, "head", 4, 2) + shift(square, "head", 4, -1)
    )
    inverse = lax.rsqrt(square.reshape(128, 1) / 2048.0 + 1e-06)
    gain = lax.dynamic_slice_in_dim(norm_gain, head * 512, 512, 0)
    normed = (hstate * inverse * gain).astype(BF)

    own_cot = lax.dynamic_slice_in_dim(cotangent, head * 512, 512, 1)
    pick, send_grads, hi, lo = route(routes.T, probs.T, own_cot)
    slot_grads = spread(exchange(send_grads))
    send_rows = jnp.dot(pick, normed, preferred_element_type=F32).astype(BF)
    slot_inputs = spread(exchange(send_rows))

    back = add_head(share(slot_grads[0], w_down, 0, slot_grads[1], w_down, 1))
    acts = [
        add_head(share(slot_inputs[e], w_gate, e, slot_inputs[e], w_up, e)) for e in range(2)
    ]
    hidden = [gather_head(hidden_share(acts[e])) for e in range(2)]
    outs = [down(hidden[e], w_down, e).reshape(64, CAP, 512) for e in range(2)]
    returning = jnp.concatenate(outs + [jnp.zeros((64, ROW - 2 * CAP, 512), BF)], 1)
    returned = exchange(returning).reshape(64 * ROW, 512)
    both = gather_head(grads_share(acts[0], acts[1], back))
    grad_down = weight_grads(hidden[0] + hidden[1], slot_grads, 1)[0]
    grad_gate, grad_up = weight_grads(both, slot_inputs, 2)
    moe = lax.dot_general(hi, returned, TN, preferred_element_type=F32) + lax.dot_general(
        lo, returned, TN, preferred_element_type=F32
    )
    layer_out = (hstate + moe).astype(BF)
    return (layer_out, grad_gate, grad_up, grad_down)


def solution(mesh):
    tok = ("ctx", "exp")
    return jax.shard_map(
        per_device,
        mesh=mesh,
        in_specs=(
            P(tok, None),
            P(tok, "head"),
            P(None, tok, "head"),
            P(None, tok),
            P("head", tok),
            P(),
            P(tok, None),
            P(tok, None),
            P(tok, None, "head"),
            P(tok, None, "head"),
            P(tok, None, "head"),
            P(tok, None),
        ),
        out_specs=(
            P(tok, "head"),
            P(tok, None, "head"),
            P(tok, None, "head"),
            P(tok, None, "head"),
        ),
        check_vma=False,
    )
```

```python
import functools
import math

import jax
import jax.numpy as jnp
from jax import lax
from jax.experimental import pallas as pl
from jax.experimental.pallas import tpu as pltpu
from jax.sharding import PartitionSpec as P

BF = jnp.bfloat16
F32 = jnp.float32
HD = 128
CAP = 10
ROW = 24
RELZ = (-1, 0, 1, -4, -3, -2, 2, 3)
NT = (((1,), (1,)), ((), ()))
TN = (((0,), (0,)), ((), ()))
ANY = pl.BlockSpec(memory_space=pl.ANY)
VM = pl.BlockSpec(memory_space=pltpu.VMEM)


def shift(x, axis, n, d):
    return lax.ppermute(x, axis, [(i, (i + d) % n) for i in range(n)])


def shift_x(x, d):
    return lax.ppermute(x, "ctx", [(i, (i + 2 * d) % 8) for i in range(8)])


def swap_core(x):
    return lax.ppermute(x, "ctx", [(i, i ^ 1) for i in range(8)])


def later(x, *others):
    return lax.optimization_barrier((x, *others))[0]


def near_z(x):
    return jnp.concatenate([shift(x, "exp", 8, 1), x, shift(x, "exp", 8, -1)], 0)


def far_z(three):
    n = three.shape[0] // 3
    far_before = shift(three, "exp", 8, 3)
    far_after = shift(three[: 2 * n], "exp", 8, -3)
    return jnp.concatenate([three, far_before, far_after], 0)


def attention_kernel(last, q_ref, qdoc_ref, *refs):
    pieces = refs[:5]
    if last:
        m_in, l_in, acc_in, o_ref, m_s, l_s, acc, kv, qs, bias, sem = refs[5:]
    else:
        m_s, l_s, acc, kv, qs, bias, sem = refs[5:]
    plan = ((0, 0, 8), (1, 0, 8), (2, 0, 8), (3, 0, 4), (3, 4, 4))
    copies = [
        pltpu.make_async_copy(pieces[p], kv.at[c, pl.ds(lo, n)], sem.at[p])
        for p, (c, lo, n) in enumerate(plan)
    ]
    for cp in copies:
        cp.start()
    ctx = lax.axis_index("ctx")
    z = lax.axis_index("exp")
    me = ctx * 8 + z
    for h in range(8):
        qs[h * 128 : (h + 1) * 128, :] = q_ref[:, h * 128 : (h + 1) * 128]
    if last:
        m_s[...] = m_in[...]
        l_s[...] = l_in[...]
        acc[...] = acc_in[...]
    else:
        m_s[...] = jnp.full(m_s.shape, -1e30, F32)
        l_s[...] = jnp.zeros(l_s.shape, F32)
        acc[...] = jnp.zeros(acc.shape, F32)
    qdoc = qdoc_ref[...].astype(F32)
    first_doc = jnp.min(qdoc)
    row = lax.broadcasted_iota(jnp.int32, (128, 128), 0)
    lane = lax.broadcasted_iota(jnp.int32, (128, 128), 1)
    coef = HD**-0.5 * math.log2(math.e)
    for cp in copies:
        cp.wait()

    def chunk(k, carry):
        dx = jnp.where(k == 1, 3, jnp.where(k == 2, 1, jnp.where(k == 3, 2, 0)))
        kcore = 1 - ctx % 2 if last else ctx % 2
        kctx = ((ctx // 2 + dx) % 4) * 2 + kcore
        docs = kv[k, :, 256:272, :].astype(F32)
        last_doc = jnp.max(docs)

        @pl.when((kctx <= ctx) & (last_doc >= first_doc))
        def _():
            for b, rel in enumerate(RELZ):
                j = kctx * 8 + (z + rel + 8) % 8
                seen = (lane + j * 128 <= row + me * 128) & (
                    docs[b, 0:1, :] == qdoc
                )
                bias[:, b * 128 : (b + 1) * 128] = jnp.where(seen, 0.0, -1e30)

            def group(g, carry2):
                r = pl.ds(pl.multiple_of(g * 256, 256), 256)
                keys = kv[k, :, 0:128, :].reshape(1024, 128)
                vals = kv[k, :, 128:256, :].reshape(1024, 128)
                s = lax.dot_general(qs[r, :], keys, NT, preferred_element_type=F32)
                s = s * coef
                s = (s.reshape(2, 128, 1024) + bias[...][None]).reshape(256, 1024)
                old = m_s[r, :]
                new = jnp.maximum(old, jnp.max(s, axis=1, keepdims=True))
                keep = jnp.exp2(old - new)
                p = jnp.exp2(s - new[:, 0:1])
                part = p[:, 0:128]
                for i in range(1, 8):
                    part = part + p[:, i * 128 : (i + 1) * 128]
                l_s[r, :] = l_s[r, :] * keep + part
                m_s[r, :] = new
                acc[r, :] = acc[r, :] * keep + lax.dot_general(
                    p.astype(BF), vals, (((1,), (0,)), ((), ())), preferred_element_type=F32
                )
                return carry2

            lax.fori_loop(0, 4, group, 0)

        return carry

    lax.fori_loop(0, 4, chunk, 0)
    if last:
        for h in range(8):
            r = slice(h * 128, (h + 1) * 128)
            whole = jnp.sum(l_s[r, :], axis=1, keepdims=True)
            o_ref[:, r] = (acc[r, :] / whole).astype(BF)


def attention(queries, doc_col, pieces, state=()):
    last = bool(state)
    flat = pltpu.VMEM((1024, 128), F32)
    return pl.pallas_call(
        functools.partial(attention_kernel, last),
        out_shape=jax.ShapeDtypeStruct((128, 1024), BF)
        if last
        else [jax.ShapeDtypeStruct((1024, 128), F32)] * 3,
        in_specs=[VM, VM] + [ANY] * 5 + [VM] * len(state),
        out_specs=VM if last else [VM] * 3,
        scratch_shapes=([flat] * 3 if last else [])
        + [
            pltpu.VMEM((4, 8, 272, 128), BF),
            pltpu.VMEM((1024, 128), BF),
            pltpu.VMEM((128, 1024), F32),
            pltpu.SemaphoreType.DMA((5,)),
        ],
        name="attention",
    )(queries, doc_col, *pieces, *state)


def project_kernel(attn_ref, *refs):
    pieces, (o0, o1, o2, o3, ws) = refs[:10], refs[10:]
    ctx = lax.axis_index("ctx")
    z = lax.axis_index("exp")
    me = lax.axis_index("head")
    own = ctx % 2
    plan = ((0, 0, 8), (3, 0, 8), (1, 0, 8), (2, 0, 4), (2, 4, 8))
    for k in range(2):
        core = own if k == 0 else 1 - own
        for p, (dx, lo, hi) in enumerate(plan):
            base = ((ctx // 2 + dx) % 4) * 512 + core * 256
            for i in range(lo, hi):
                at = base + ((z + RELZ[i] + 8) % 8) * 32
                ws[pl.ds(pl.multiple_of(at, 32), 32), :] = pieces[k * 5 + p][
                    (i - lo) * 32 : (i - lo + 1) * 32, :
                ]
    for d, out in enumerate((o0, o1, o2, o3)):
        at = pl.multiple_of(((me + d) % 4) * 512, 512)
        part = lax.dot_general(
            attn_ref[...], ws[pl.ds(at, 512), :], NT, preferred_element_type=F32
        )
        out[...] = part.astype(out.dtype)


def project(attn, pieces):
    return pl.pallas_call(
        project_kernel,
        out_shape=[jax.ShapeDtypeStruct((128, 512), F32)]
        + [jax.ShapeDtypeStruct((128, 512), BF)] * 3,
        in_specs=[VM] * 11,
        out_specs=[VM] * 4,
        scratch_shapes=[pltpu.VMEM((2048, 1024), BF)],
        name="project",
    )(attn, *pieces)


def route_kernel(routes_ref, probs_ref, cot_ref, pick_ref, grad_ref, hi_ref, lo_ref):
    expert = lax.broadcasted_iota(jnp.int32, (128, 128), 0)
    named = jnp.zeros((128, 128), F32)
    weight = jnp.zeros((128, 128), F32)
    for k in range(8):
        hit = routes_ref[k : k + 1, :] == expert
        named = named + jnp.where(hit, 1.0, 0.0)
        weight = weight + jnp.where(hit, probs_ref[k : k + 1, :], 0.0)
    earlier = (
        lax.broadcasted_iota(jnp.int32, (128, 128), 0)
        < lax.broadcasted_iota(jnp.int32, (128, 128), 1)
    )
    rank = jnp.dot(
        named.astype(BF),
        jnp.where(earlier, 1.0, 0.0).astype(BF),
        preferred_element_type=F32,
    )
    place = (named * (rank + 1.0)).astype(BF)
    w1 = weight.astype(BF)
    rest = weight - w1.astype(F32)
    w2 = rest.astype(BF)
    w3 = (rest - w2.astype(F32)).astype(BF)
    size = 384
    for part in range(4):
        r = lax.broadcasted_iota(jnp.int32, (size, 128), 0)
        owner = jnp.zeros((size, 128), jnp.int32)
        for o in range(1, 16):
            owner = owner + jnp.where(r >= o * ROW, 1, 0)
        inner = r - owner * ROW
        second = jnp.where(inner >= CAP, 1, 0)
        slot = inner - second * CAP
        slot = jnp.where(inner >= 2 * CAP, 1000, slot)
        of = (owner + part * 16) * 2 + second
        chosen = jnp.where(
            of == lax.broadcasted_iota(jnp.int32, (size, 128), 1), 1.0, 0.0
        ).astype(BF)
        dot = functools.partial(jnp.dot, preferred_element_type=F32)
        mine = dot(chosen, place) == (slot + 1).astype(F32)
        w = (dot(chosen, w1) + dot(chosen, w2)) + dot(chosen, w3)
        w = jnp.where(mine, w, 0.0)
        pick = jnp.where(mine, 1.0, 0.0).astype(BF)
        at = slice(part * size, (part + 1) * size)
        pick_ref[at, :] = pick
        scale = jnp.sum(w, axis=1, keepdims=True)
        grad_ref[at, :] = (scale * dot(pick, cot_ref[...])).astype(BF)
        hi = w.astype(BF)
        hi_ref[at, :] = hi
        lo_ref[at, :] = (w - hi.astype(F32)).astype(BF)


def route(routes_t, probs_t, cot):
    rows = 64 * ROW
    sq = jax.ShapeDtypeStruct((rows, 128), BF)
    return pl.pallas_call(
        route_kernel,
        out_shape=[sq, jax.ShapeDtypeStruct((rows, 512), BF), sq, sq],
        in_specs=[VM] * 3,
        out_specs=[VM] * 4,
        name="route",
    )(routes_t, probs_t, cot)


def pull(got_ref, e):
    return got_ref[:, e * CAP : (e + 1) * CAP, :].reshape(640, 512)


def share_kernel(ea, eb, got_ref, wa_ref, wb_ref, own, up, down, keep1, keep3, s, x):
    me = lax.axis_index("head")
    step = pl.program_id(0)

    @pl.when(step == 0)
    def _():
        x[...] = pull(got_ref, ea)

    if eb != ea:

        @pl.when(step == 1)
        def _():
            x[...] = pull(got_ref, eb)

    w = jnp.where(step == 0, wa_ref[...], wb_ref[...])
    s[...] = lax.dot_general(x[...], w, NT, preferred_element_type=F32)

    def rows(d, lo, n):
        at = pl.multiple_of(((me + d) % 4) * 160 + lo, 16)
        return s[pl.ds(at, n), :]

    own[...] = rows(0, 0, 160)
    up[0:80, :] = rows(2, 0, 80).astype(BF)
    up[80:160, :] = rows(1, 80, 80).astype(BF)
    down[0:80, :] = rows(2, 80, 80).astype(BF)
    down[80:160, :] = rows(3, 0, 80).astype(BF)
    keep1[...] = rows(1, 0, 80)
    keep3[...] = rows(3, 80, 80)


def share(got, wa, ia, wb, ib):
    shapes = [(160, F32), (160, BF), (160, BF), (80, F32), (80, F32)]
    return pl.pallas_call(
        functools.partial(share_kernel, ia, ib),
        out_shape=[jax.ShapeDtypeStruct((n, 1536), t) for n, t in shapes],
        grid=(2,),
        in_specs=[
            pl.BlockSpec((64, ROW, 512), lambda g: (0, 0, 0)),
            pl.BlockSpec((None, 768, 512), lambda g: (ia, 0, 0)),
            pl.BlockSpec((None, 768, 512), lambda g: (ib, 0, 0)),
        ],
        out_specs=[pl.BlockSpec((n, 768), lambda g: (0, g)) for n, t in shapes],
        scratch_shapes=[pltpu.VMEM((640, 768), F32), pltpu.VMEM((640, 512), BF)],
        name="share",
    )(got, wa, wb)


def add_head(parts):
    own, up, down, keep1, keep3 = parts
    below, above = shift(up, "head", 4, 1), shift(down, "head", 4, -1)
    relay1 = (keep1 + below[:80].astype(F32)).astype(BF)
    relay3 = (keep3 + above[:80].astype(F32)).astype(BF)
    far1, far3 = shift(relay1, "head", 4, 1), shift(relay3, "head", 4, -1)
    return own, below, above, far1, far3


def total(own, below, above, far1, far3, cols):
    lo = (own[0:80, cols] + above[80:160, cols].astype(F32)) + far1[:, cols].astype(F32)
    hi = (own[80:160, cols] + below[80:160, cols].astype(F32)) + far3[:, cols].astype(F32)
    return lo, hi


def hidden_kernel(*refs):
    acts, hidden = refs[:5], refs[5]
    for c in range(0, 768, 384):
        gates = total(*acts, slice(c, c + 384))
        ups = total(*acts, slice(768 + c, 768 + c + 384))
        for i in range(2):
            sigma = 1.0 / (1.0 + jnp.exp(-gates[i]))
            hidden[i * 80 : (i + 1) * 80, c : c + 384] = (gates[i] * sigma * ups[i]).astype(BF)


def hidden_share(acts):
    return pl.pallas_call(
        hidden_kernel,
        out_shape=jax.ShapeDtypeStruct((160, 768), BF),
        in_specs=[VM] * 5,
        out_specs=VM,
        name="hidden",
    )(*acts)


def grads_kernel(e, *refs):
    acts, grad, grads = refs[:5], refs[5:10], refs[10]
    for c in range(0, 768, 384):
        gates = total(*acts, slice(c, c + 384))
        ups = total(*acts, slice(768 + c, 768 + c + 384))
        back = total(*grad, slice(e * 768 + c, e * 768 + c + 384))
        for i in range(2):
            r = slice(i * 80, (i + 1) * 80)
            sigma = 1.0 / (1.0 + jnp.exp(-gates[i]))
            gg = back[i] * ups[i] * sigma * (1.0 + gates[i] * (1.0 - sigma))
            grads[r, c : c + 384] = gg.astype(BF)
            grads[r, 768 + c : 768 + c + 384] = (back[i] * (gates[i] * sigma)).astype(BF)


def grads_share(e, acts, grad):
    return pl.pallas_call(
        functools.partial(grads_kernel, e),
        out_shape=jax.ShapeDtypeStruct((160, 1536), BF),
        in_specs=[VM] * 10,
        out_specs=VM,
        name="grads",
    )(*acts, *grad)


def gather_head(x):
    below, above = shift(x, "head", 4, 1), shift(x, "head", 4, -1)
    far_a, far_b = shift(below[:80], "head", 4, 1), shift(above[80:], "head", 4, -1)
    return x, below, above, far_a, far_b


def assemble(me, refs, out, cols):
    x, below, above, far_a, far_b = refs
    for d, lo, n, ref in (
        (0, 0, 160, x),
        (3, 0, 160, below),
        (1, 0, 160, above),
        (2, 0, 80, far_a),
        (2, 80, 80, far_b),
    ):
        at = pl.multiple_of(((me + d) % 4) * 160 + lo, 16)
        out[pl.ds(at, n), :] = ref[:, cols]


def down_kernel(*refs):
    w_ref, out, h = refs[10:]
    me = lax.axis_index("head")
    for e in range(2):
        assemble(me, refs[e * 5 : e * 5 + 5], h, slice(0, 768))
        y = jnp.dot(h[...], w_ref[e], preferred_element_type=F32).astype(BF)
        out[:, e * CAP : (e + 1) * CAP, :] = y.reshape(64, CAP, 512)
    out[:, 2 * CAP : ROW, :] = jnp.zeros((64, ROW - 2 * CAP, 512), BF)


def down(hidden, w_down):
    return pl.pallas_call(
        down_kernel,
        out_shape=jax.ShapeDtypeStruct((64, ROW, 512), BF),
        in_specs=[VM] * 11,
        out_specs=VM,
        scratch_shapes=[pltpu.VMEM((640, 768), BF)],
        name="down",
    )(*hidden[0], *hidden[1], w_down)


def weight_grad_kernel(n_out, *refs):
    n = 10 * n_out
    me = lax.axis_index("head")
    first = pl.program_id(0) == 0
    pieces, got, outs, (t, x) = refs[:n], refs[n], refs[n + 1 : -2], refs[-2:]

    for e in range(2):
        now = first if e == 0 else jnp.logical_not(first)

        @pl.when(now & (pl.program_id(1) == 0))
        def _():
            x[...] = pull(got, e)

    for k in range(n_out):
        for e in range(2):

            @pl.when(first if e == 0 else jnp.logical_not(first))
            def _():
                at = (k * 2 + e) * 5
                assemble(me, pieces[at : at + 5], t, slice(0, 256))

        outs[k][...] = lax.dot_general(
            t[...], x[...], TN, preferred_element_type=F32
        ).astype(BF)


def weight_grads(sets, got):
    args, specs = [], []
    for per_expert in sets:
        for e, (pieces, col) in enumerate(per_expert):
            for a in pieces:
                args.append(a)
                specs.append(
                    pl.BlockSpec(
                        (a.shape[0], 256),
                        lambda g, f, col=col, e=e: (0, col + jnp.where(g == e, f, 0)),
                    )
                )
    n_out = len(sets)
    return pl.pallas_call(
        functools.partial(weight_grad_kernel, n_out),
        out_shape=[jax.ShapeDtypeStruct((2, 768, 512), BF)] * n_out,
        grid=(2, 3),
        in_specs=specs + [pl.BlockSpec((64, ROW, 512), lambda g, f: (0, 0, 0))],
        out_specs=[pl.BlockSpec((None, 256, 512), lambda g, f: (g, f, 0))] * n_out,
        scratch_shapes=[pltpu.VMEM((640, 256), BF), pltpu.VMEM((640, 512), BF)],
        name="weight_grads",
    )(*args, got)


def exchange(x):
    return lax.all_to_all(
        x.reshape(64, ROW, 512), ("ctx", "exp"), split_axis=0, concat_axis=0, tiled=True
    )


def per_device(
    resid,
    queries,
    rotated_key_value_pairs,
    doc_ids,
    out_weight,
    norm_gain,
    routes,
    probs,
    w_gate,
    w_up,
    w_down,
    cotangent,
):
    head = lax.axis_index("head")
    packed = jnp.concatenate(
        [
            rotated_key_value_pairs.reshape(256, 128),
            jnp.broadcast_to(doc_ids.astype(BF), (16, 128)),
        ],
        0,
    )
    own_cot = lax.dynamic_slice_in_dim(cotangent, head * 512, 512, 1)
    pick, send_grads, hi, lo = route(routes.T, probs.T, own_cot)
    wthree = near_z(out_weight.T)
    three = later(near_z(packed), pick, wthree)
    z0 = far_z(three).reshape(8, 272, 128)
    below, above = shift_x(z0, 1), shift_x(z0, -1)
    w0 = far_z(later(wthree, z0))
    far_a = shift_x(later(below, w0)[:4], 1)
    far_b = shift_x(later(above, w0)[4:], -1)
    pieces = (z0, below, above, far_a, far_b)
    doc_col = doc_ids.reshape(128, 1)
    w0 = later(w0, far_a, far_b)
    wbelow, wabove = shift_x(w0, 1), shift_x(w0, -1)
    swapped = tuple(swap_core(p) for p in pieces)
    state = attention(queries, doc_col, pieces)
    wfar_a = shift_x(later(wbelow, *state)[:128], 1)
    wfar_b = shift_x(later(wabove, *state)[128:], -1)
    attn = attention(later(queries, wbelow, wabove), doc_col, swapped, state)
    w_pieces = (w0, wbelow, wabove, wfar_a, wfar_b)
    w_pieces = w_pieces + tuple(swap_core(later(p, *state)) for p in w_pieces)
    o0, o1, o2, o3 = project(attn, w_pieces)
    attn_sum = (o0 + shift(o1, "head", 4, 1).astype(F32)) + (
        shift(o2, "head", 4, 2).astype(F32) + shift(o3, "head", 4, -1).astype(F32)
    )
    own_resid = lax.dynamic_slice_in_dim(resid, head * 512, 512, 1)
    hstate = (own_resid.astype(F32) + attn_sum).astype(BF).astype(F32)
    square = jnp.sum(hstate * hstate, axis=-1).reshape(1, 128)
    square = (square + shift(square, "head", 4, 1)) + (
        shift(square, "head", 4, 2) + shift(square, "head", 4, -1)
    )
    inverse = lax.rsqrt(square.reshape(128, 1) / 2048.0 + 1e-06)
    gain = lax.dynamic_slice_in_dim(norm_gain, head * 512, 512, 0)
    normed = (hstate * inverse * gain).astype(BF)

    send_rows = jnp.dot(pick, normed, preferred_element_type=F32).astype(BF)
    got_rows = exchange(send_rows)
    terms = [share(got_rows, w_gate, e, w_up, e) for e in range(2)]
    acts = [add_head(terms[e]) for e in range(2)]
    got_grads = exchange(later(send_grads, terms[0][0], terms[1][0]))
    hidden = [gather_head(hidden_share(acts[e])) for e in range(2)]
    back_terms = share(later(got_grads, hidden[1][0]), w_down, 0, w_down, 1)
    back = add_head(back_terms)
    held = tuple(later(a, back_terms[3]) for a in hidden[0])
    returned = exchange(down((held, hidden[1]), w_down)).reshape(64 * ROW, 512)
    both = [gather_head(grads_share(e, acts[e], back)) for e in range(2)]
    (grad_down,) = weight_grads([[(hidden[e], 0) for e in range(2)]], got_grads)
    grad_gate, grad_up = weight_grads(
        [[(both[e], 0) for e in range(2)], [(both[e], 3) for e in range(2)]], got_rows
    )
    moe = lax.dot_general(hi, returned, TN, preferred_element_type=F32) + lax.dot_general(
        lo, returned, TN, preferred_element_type=F32
    )
    layer_out = (hstate + moe).astype(BF)
    return (layer_out, grad_gate, grad_up, grad_down)


def solution(mesh):
    tok = ("ctx", "exp")
    return jax.shard_map(
        per_device,
        mesh=mesh,
        in_specs=(
            P(tok, None),
            P(tok, "head"),
            P(None, tok, "head"),
            P(None, tok),
            P("head", tok),
            P(),
            P(tok, None),
            P(tok, None),
            P(tok, None, "head"),
            P(tok, None, "head"),
            P(tok, None, "head"),
            P(tok, None),
        ),
        out_specs=(
            P(tok, "head"),
            P(tok, None, "head"),
            P(tok, None, "head"),
            P(tok, None, "head"),
        ),
        check_vma=False,
    )
```

```python
import functools
import math

import jax
import jax.numpy as jnp
from jax import lax
from jax.experimental import pallas as pl
from jax.experimental.pallas import tpu as pltpu
from jax.sharding import PartitionSpec as P


BF = jnp.bfloat16
F32 = jnp.float32
HD = 128
CAP = 10
ROW = 24
RELZ = (-1, 0, 1, -4, -3, -2, 2, 3)
NT = (((1,), (1,)), ((), ()))
TN = (((0,), (0,)), ((), ()))
ANY = pl.BlockSpec(memory_space=pl.ANY)
VM = pl.BlockSpec(memory_space=pltpu.VMEM)


def shift(x, axis, n, d):
    return lax.ppermute(x, axis, [(i, (i + d) % n) for i in range(n)])


def shift_x(x, d):
    return lax.ppermute(x, "ctx", [(i, (i + 2 * d) % 8) for i in range(8)])


def swap_core(x):
    return lax.ppermute(x, "ctx", [(i, i ^ 1) for i in range(8)])


def later(x, *others):
    return lax.optimization_barrier((x, *others))[0]


def near_z(x):
    return jnp.concatenate([shift(x, "exp", 8, 1), x, shift(x, "exp", 8, -1)], 0)


def far_z(three):
    n = three.shape[0] // 3
    far_before = shift(three, "exp", 8, 3)
    far_after = shift(three[: 2 * n], "exp", 8, -3)
    return jnp.concatenate([three, far_before, far_after], 0)


def attention_kernel(last, q_ref, qdoc_ref, *refs):
    pieces = refs[:5]
    if last:
        m_in, l_in, acc_in, o_ref, m_s, l_s, acc, kv, qs, bias, sem = refs[5:]
    else:
        m_s, l_s, acc, kv, qs, bias, sem = refs[5:]
    plan = ((0, 0, 8), (1, 0, 8), (2, 0, 8), (3, 0, 4), (3, 4, 4))
    copies = [
        pltpu.make_async_copy(pieces[p], kv.at[c, pl.ds(lo, n)], sem.at[p])
        for p, (c, lo, n) in enumerate(plan)
    ]
    for cp in copies:
        cp.start()
    ctx = lax.axis_index("ctx")
    z = lax.axis_index("exp")
    me = ctx * 8 + z
    for h in range(8):
        qs[h * 128 : (h + 1) * 128, :] = q_ref[:, h * 128 : (h + 1) * 128]
    if last:
        m_s[...] = m_in[...]
        l_s[...] = l_in[...]
        acc[...] = acc_in[...]
    else:
        m_s[...] = jnp.full(m_s.shape, -1e30, F32)
        l_s[...] = jnp.zeros(l_s.shape, F32)
        acc[...] = jnp.zeros(acc.shape, F32)
    qdoc = qdoc_ref[...].astype(F32)
    first_doc = jnp.min(qdoc)
    row = lax.broadcasted_iota(jnp.int32, (128, 128), 0)
    lane = lax.broadcasted_iota(jnp.int32, (128, 128), 1)
    coef = HD**-0.5 * math.log2(math.e)
    for cp in copies:
        cp.wait()

    def chunk(k, carry):
        dx = jnp.where(k == 1, 3, jnp.where(k == 2, 1, jnp.where(k == 3, 2, 0)))
        kcore = 1 - ctx % 2 if last else ctx % 2
        kctx = ((ctx // 2 + dx) % 4) * 2 + kcore
        docs = kv[k, :, 256:272, :].astype(F32)
        last_doc = jnp.max(docs)

        @pl.when((kctx <= ctx) & (last_doc >= first_doc))
        def _():
            for b, rel in enumerate(RELZ):
                j = kctx * 8 + (z + rel + 8) % 8
                seen = (lane + j * 128 <= row + me * 128) & (
                    docs[b, 0:1, :] == qdoc
                )
                bias[:, b * 128 : (b + 1) * 128] = jnp.where(seen, 0.0, -1e30)

            def group(g, carry2):
                r = pl.ds(pl.multiple_of(g * 256, 256), 256)
                keys = kv[k, :, 0:128, :].reshape(1024, 128)
                vals = kv[k, :, 128:256, :].reshape(1024, 128)
                s = lax.dot_general(qs[r, :], keys, NT, preferred_element_type=F32)
                s = s * coef
                s = (s.reshape(2, 128, 1024) + bias[...][None]).reshape(256, 1024)
                old = m_s[r, :]
                new = jnp.maximum(old, jnp.max(s, axis=1, keepdims=True))
                keep = jnp.exp2(old - new)
                p = jnp.exp2(s - new[:, 0:1])
                part = p[:, 0:128]
                for i in range(1, 8):
                    part = part + p[:, i * 128 : (i + 1) * 128]
                l_s[r, :] = l_s[r, :] * keep + part
                m_s[r, :] = new
                acc[r, :] = acc[r, :] * keep + lax.dot_general(
                    p.astype(BF), vals, (((1,), (0,)), ((), ())), preferred_element_type=F32
                )
                return carry2

            lax.fori_loop(0, 4, group, 0)

        return carry

    lax.fori_loop(0, 4, chunk, 0)
    if last:
        for h in range(8):
            r = slice(h * 128, (h + 1) * 128)
            whole = jnp.sum(l_s[r, :], axis=1, keepdims=True)
            o_ref[:, r] = (acc[r, :] / whole).astype(BF)


def attention(queries, doc_col, pieces, state=()):
    last = bool(state)
    flat = pltpu.VMEM((1024, 128), F32)
    return pl.pallas_call(
        functools.partial(attention_kernel, last),
        out_shape=jax.ShapeDtypeStruct((128, 1024), BF)
        if last
        else [jax.ShapeDtypeStruct((1024, 128), F32)] * 3,
        in_specs=[VM, VM] + [ANY] * 5 + [VM] * len(state),
        out_specs=VM if last else [VM] * 3,
        scratch_shapes=([flat] * 3 if last else [])
        + [
            pltpu.VMEM((4, 8, 272, 128), BF),
            pltpu.VMEM((1024, 128), BF),
            pltpu.VMEM((128, 1024), F32),
            pltpu.SemaphoreType.DMA((5,)),
        ],
        name="attention",
    )(queries, doc_col, *pieces, *state)


def project_kernel(attn_ref, *refs):
    pieces, (o0, o1, o2, o3, ws) = refs[:10], refs[10:]
    ctx = lax.axis_index("ctx")
    z = lax.axis_index("exp")
    me = lax.axis_index("head")
    own = ctx % 2
    plan = ((0, 0, 8), (3, 0, 8), (1, 0, 8), (2, 0, 4), (2, 4, 8))
    for k in range(2):
        core = own if k == 0 else 1 - own
        for p, (dx, lo, hi) in enumerate(plan):
            base = ((ctx // 2 + dx) % 4) * 512 + core * 256
            for i in range(lo, hi):
                at = base + ((z + RELZ[i] + 8) % 8) * 32
                ws[pl.ds(pl.multiple_of(at, 32), 32), :] = pieces[k * 5 + p][
                    (i - lo) * 32 : (i - lo + 1) * 32, :
                ]
    for d, out in enumerate((o0, o1, o2, o3)):
        at = pl.multiple_of(((me + d) % 4) * 512, 512)
        part = lax.dot_general(
            attn_ref[...], ws[pl.ds(at, 512), :], NT, preferred_element_type=F32
        )
        out[...] = part.astype(out.dtype)


def project(attn, pieces):
    return pl.pallas_call(
        project_kernel,
        out_shape=[jax.ShapeDtypeStruct((128, 512), F32)]
        + [jax.ShapeDtypeStruct((128, 512), BF)] * 3,
        in_specs=[VM] * 11,
        out_specs=[VM] * 4,
        scratch_shapes=[pltpu.VMEM((2048, 1024), BF)],
        name="project",
    )(attn, *pieces)


def route_kernel(routes_ref, probs_ref, cot_ref, pick_ref, grad_ref, hi_ref, lo_ref):
    expert = lax.broadcasted_iota(jnp.int32, (128, 128), 0)
    named = jnp.zeros((128, 128), F32)
    weight = jnp.zeros((128, 128), F32)
    for k in range(8):
        hit = routes_ref[k : k + 1, :] == expert
        named = named + jnp.where(hit, 1.0, 0.0)
        weight = weight + jnp.where(hit, probs_ref[k : k + 1, :], 0.0)
    earlier = (
        lax.broadcasted_iota(jnp.int32, (128, 128), 0)
        < lax.broadcasted_iota(jnp.int32, (128, 128), 1)
    )
    rank = jnp.dot(
        named.astype(BF),
        jnp.where(earlier, 1.0, 0.0).astype(BF),
        preferred_element_type=F32,
    )
    place = (named * (rank + 1.0)).astype(BF)
    w1 = weight.astype(BF)
    rest = weight - w1.astype(F32)
    w2 = rest.astype(BF)
    w3 = (rest - w2.astype(F32)).astype(BF)
    size = 384
    for part in range(4):
        r = lax.broadcasted_iota(jnp.int32, (size, 128), 0)
        owner = jnp.zeros((size, 128), jnp.int32)
        for o in range(1, 16):
            owner = owner + jnp.where(r >= o * ROW, 1, 0)
        inner = r - owner * ROW
        second = jnp.where(inner >= CAP, 1, 0)
        slot = inner - second * CAP
        slot = jnp.where(inner >= 2 * CAP, 1000, slot)
        of = (owner + part * 16) * 2 + second
        chosen = jnp.where(
            of == lax.broadcasted_iota(jnp.int32, (size, 128), 1), 1.0, 0.0
        ).astype(BF)
        dot = functools.partial(jnp.dot, preferred_element_type=F32)
        mine = dot(chosen, place) == (slot + 1).astype(F32)
        w = (dot(chosen, w1) + dot(chosen, w2)) + dot(chosen, w3)
        w = jnp.where(mine, w, 0.0)
        pick = jnp.where(mine, 1.0, 0.0).astype(BF)
        at = slice(part * size, (part + 1) * size)
        pick_ref[at, :] = pick
        scale = jnp.sum(w, axis=1, keepdims=True)
        grad_ref[at, :] = (scale * dot(pick, cot_ref[...])).astype(BF)
        hi = w.astype(BF)
        hi_ref[at, :] = hi
        lo_ref[at, :] = (w - hi.astype(F32)).astype(BF)


def route(routes_t, probs_t, cot):
    rows = 64 * ROW
    sq = jax.ShapeDtypeStruct((rows, 128), BF)
    return pl.pallas_call(
        route_kernel,
        out_shape=[sq, jax.ShapeDtypeStruct((rows, 512), BF), sq, sq],
        in_specs=[VM] * 3,
        out_specs=[VM] * 4,
        name="route",
    )(routes_t, probs_t, cot)


def pull(got_ref, e):
    return got_ref[:, e * CAP : (e + 1) * CAP, :].reshape(640, 512)


def share_kernel(ea, eb, got_ref, wa_ref, wb_ref, own, up, down, keep1, keep3, s, x):
    me = lax.axis_index("head")
    step = pl.program_id(0)

    @pl.when(step == 0)
    def _():
        x[...] = pull(got_ref, ea)

    if eb != ea:

        @pl.when(step == 1)
        def _():
            x[...] = pull(got_ref, eb)

    w = jnp.where(step == 0, wa_ref[...], wb_ref[...])
    s[...] = lax.dot_general(x[...], w, NT, preferred_element_type=F32)

    def rows(d, lo, n):
        at = pl.multiple_of(((me + d) % 4) * 160 + lo, 16)
        return s[pl.ds(at, n), :]

    own[...] = rows(0, 0, 160)
    up[0:80, :] = rows(2, 0, 80).astype(BF)
    up[80:160, :] = rows(1, 80, 80).astype(BF)
    down[0:80, :] = rows(2, 80, 80).astype(BF)
    down[80:160, :] = rows(3, 0, 80).astype(BF)
    keep1[...] = rows(1, 0, 80)
    keep3[...] = rows(3, 80, 80)


def share(got, wa, ia, wb, ib):
    shapes = [(160, F32), (160, BF), (160, BF), (80, F32), (80, F32)]
    return pl.pallas_call(
        functools.partial(share_kernel, ia, ib),
        out_shape=[jax.ShapeDtypeStruct((n, 1536), t) for n, t in shapes],
        grid=(2,),
        in_specs=[
            pl.BlockSpec((64, ROW, 512), lambda g: (0, 0, 0)),
            pl.BlockSpec((None, 768, 512), lambda g: (ia, 0, 0)),
            pl.BlockSpec((None, 768, 512), lambda g: (ib, 0, 0)),
        ],
        out_specs=[pl.BlockSpec((n, 768), lambda g: (0, g)) for n, t in shapes],
        scratch_shapes=[pltpu.VMEM((640, 768), F32), pltpu.VMEM((640, 512), BF)],
        name="share",
    )(got, wa, wb)


def add_head(parts):
    own, up, down, keep1, keep3 = parts
    below, above = shift(up, "head", 4, 1), shift(down, "head", 4, -1)
    relay1 = (keep1 + below[:80].astype(F32)).astype(BF)
    relay3 = (keep3 + above[:80].astype(F32)).astype(BF)
    far1, far3 = shift(relay1, "head", 4, 1), shift(relay3, "head", 4, -1)
    return own, below, above, far1, far3


def total(own, below, above, far1, far3, cols):
    lo = (own[0:80, cols] + above[80:160, cols].astype(F32)) + far1[:, cols].astype(F32)
    hi = (own[80:160, cols] + below[80:160, cols].astype(F32)) + far3[:, cols].astype(F32)
    return lo, hi


def active_kernel(e, *refs):
    acts, grad, (hidden, grads) = refs[:5], refs[5:10], refs[10:]
    for c in range(0, 768, 384):
        gates = total(*acts, slice(c, c + 384))
        ups = total(*acts, slice(768 + c, 768 + c + 384))
        back = total(*grad, slice(e * 768 + c, e * 768 + c + 384))
        for i in range(2):
            r = slice(i * 80, (i + 1) * 80)
            sigma = 1.0 / (1.0 + jnp.exp(-gates[i]))
            silu = gates[i] * sigma
            hidden[r, c : c + 384] = (silu * ups[i]).astype(BF)
            gg = back[i] * ups[i] * sigma * (1.0 + gates[i] * (1.0 - sigma))
            grads[r, c : c + 384] = gg.astype(BF)
            grads[r, 768 + c : 768 + c + 384] = (back[i] * silu).astype(BF)


def active(e, acts, grad):
    return pl.pallas_call(
        functools.partial(active_kernel, e),
        out_shape=[
            jax.ShapeDtypeStruct((160, 768), BF),
            jax.ShapeDtypeStruct((160, 1536), BF),
        ],
        in_specs=[VM] * 10,
        out_specs=[VM] * 2,
        name="active",
    )(*acts, *grad)


def gather_head(x):
    below, above = shift(x, "head", 4, 1), shift(x, "head", 4, -1)
    far_a, far_b = shift(below[:80], "head", 4, 1), shift(above[80:], "head", 4, -1)
    return x, below, above, far_a, far_b


def assemble(me, refs, out, cols):
    x, below, above, far_a, far_b = refs
    for d, lo, n, ref in (
        (0, 0, 160, x),
        (3, 0, 160, below),
        (1, 0, 160, above),
        (2, 0, 80, far_a),
        (2, 80, 80, far_b),
    ):
        at = pl.multiple_of(((me + d) % 4) * 160 + lo, 16)
        out[pl.ds(at, n), :] = ref[:, cols]


def down_kernel(*refs):
    w_ref, out, h = refs[10:]
    me = lax.axis_index("head")
    for e in range(2):
        assemble(me, refs[e * 5 : e * 5 + 5], h, slice(0, 768))
        y = jnp.dot(h[...], w_ref[e], preferred_element_type=F32).astype(BF)
        out[:, e * CAP : (e + 1) * CAP, :] = y.reshape(64, CAP, 512)
    out[:, 2 * CAP : ROW, :] = jnp.zeros((64, ROW - 2 * CAP, 512), BF)


def down(hidden, w_down):
    return pl.pallas_call(
        down_kernel,
        out_shape=jax.ShapeDtypeStruct((64, ROW, 512), BF),
        in_specs=[VM] * 11,
        out_specs=VM,
        scratch_shapes=[pltpu.VMEM((640, 768), BF)],
        name="down",
    )(*hidden[0], *hidden[1], w_down)


def weight_grad_kernel(n_out, *refs):
    n = 10 * n_out
    me = lax.axis_index("head")
    first = pl.program_id(0) == 0
    pieces, got, outs, (t, x) = refs[:n], refs[n], refs[n + 1 : -2], refs[-2:]

    for e in range(2):
        now = first if e == 0 else jnp.logical_not(first)

        @pl.when(now & (pl.program_id(1) == 0))
        def _():
            x[...] = pull(got, e)

    for k in range(n_out):
        for e in range(2):

            @pl.when(first if e == 0 else jnp.logical_not(first))
            def _():
                at = (k * 2 + e) * 5
                assemble(me, pieces[at : at + 5], t, slice(0, 256))

        outs[k][...] = lax.dot_general(
            t[...], x[...], TN, preferred_element_type=F32
        ).astype(BF)


def weight_grads(sets, got):
    args, specs = [], []
    for per_expert in sets:
        for e, (pieces, col) in enumerate(per_expert):
            for a in pieces:
                args.append(a)
                specs.append(
                    pl.BlockSpec(
                        (a.shape[0], 256),
                        lambda g, f, col=col, e=e: (0, col + jnp.where(g == e, f, 0)),
                    )
                )
    n_out = len(sets)
    return pl.pallas_call(
        functools.partial(weight_grad_kernel, n_out),
        out_shape=[jax.ShapeDtypeStruct((2, 768, 512), BF)] * n_out,
        grid=(2, 3),
        in_specs=specs + [pl.BlockSpec((64, ROW, 512), lambda g, f: (0, 0, 0))],
        out_specs=[pl.BlockSpec((None, 256, 512), lambda g, f: (g, f, 0))] * n_out,
        scratch_shapes=[pltpu.VMEM((640, 256), BF), pltpu.VMEM((640, 512), BF)],
        name="weight_grads",
    )(*args, got)


def exchange(x):
    return lax.all_to_all(
        x.reshape(64, ROW, 512), ("ctx", "exp"), split_axis=0, concat_axis=0, tiled=True
    )


def per_device(
    resid,
    queries,
    rotated_key_value_pairs,
    doc_ids,
    out_weight,
    norm_gain,
    routes,
    probs,
    w_gate,
    w_up,
    w_down,
    cotangent,
):
    head = lax.axis_index("head")
    packed = jnp.concatenate(
        [
            rotated_key_value_pairs.reshape(256, 128),
            jnp.broadcast_to(doc_ids.astype(BF), (16, 128)),
        ],
        0,
    )
    own_cot = lax.dynamic_slice_in_dim(cotangent, head * 512, 512, 1)
    pick, send_grads, hi, lo = route(routes.T, probs.T, own_cot)
    wthree = near_z(out_weight.T)
    three = later(near_z(packed), pick, wthree)
    z0 = far_z(three).reshape(8, 272, 128)
    below, above = shift_x(z0, 1), shift_x(z0, -1)
    z0_swapped = swap_core(z0)
    w0 = far_z(later(wthree, z0))
    far_a = shift_x(later(below, w0, z0_swapped)[:4], 1)
    far_b = shift_x(later(above, w0, z0_swapped)[4:], -1)
    pieces = (z0, below, above, far_a, far_b)
    doc_col = doc_ids.reshape(128, 1)
    w0 = later(w0, far_a, far_b)
    wbelow = shift_x(w0, 1)
    wabove = shift_x(w0, -1)
    swapped = [z0_swapped]
    for p in pieces[1:]:
        swapped.append(swap_core(p))
    state = attention(queries, doc_col, pieces)
    wfar_a = shift_x(later(wbelow, *state)[:128], 1)
    wfar_b = shift_x(later(wabove, *state)[128:], -1)
    got_grads = exchange(later(send_grads, wbelow, wabove, *state))
    attn = attention(later(queries, wbelow, wabove), doc_col, swapped, state)
    w_pieces = (w0, wbelow, wabove, wfar_a, wfar_b)
    w_pieces = w_pieces + tuple(swap_core(later(p, *state)) for p in w_pieces)
    o0, o1, o2, o3 = project(attn, w_pieces)
    attn_sum = (o0 + shift(o1, "head", 4, 1).astype(F32)) + (
        shift(o2, "head", 4, 2).astype(F32) + shift(o3, "head", 4, -1).astype(F32)
    )
    own_resid = lax.dynamic_slice_in_dim(resid, head * 512, 512, 1)
    hstate = (own_resid.astype(F32) + attn_sum).astype(BF).astype(F32)
    square = jnp.sum(hstate * hstate, axis=-1).reshape(1, 128)
    square = (square + shift(square, "head", 4, 1)) + (
        shift(square, "head", 4, 2) + shift(square, "head", 4, -1)
    )
    inverse = lax.rsqrt(square.reshape(128, 1) / 2048.0 + 1e-06)
    gain = lax.dynamic_slice_in_dim(norm_gain, head * 512, 512, 0)
    normed = (hstate * inverse * gain).astype(BF)

    send_rows = jnp.dot(pick, normed, preferred_element_type=F32).astype(BF)
    got_rows = exchange(send_rows)
    back = add_head(share(later(got_grads, send_rows), w_down, 0, w_down, 1))
    got_rows = later(got_rows, *back[1:])
    terms = [share(got_rows, w_gate, e, w_up, e) for e in range(2)]
    acts = [add_head(terms[e]) for e in range(2)]
    shares = [active(e, acts[e], back) for e in range(2)]
    hidden = [gather_head(shares[e][0]) for e in range(2)]
    returned = exchange(down(hidden, w_down)).reshape(64 * ROW, 512)
    both = [gather_head(later(shares[e][1], hidden[1][1], hidden[0][1])) for e in range(2)]
    (grad_down,) = weight_grads([[(hidden[e], 0) for e in range(2)]], got_grads)
    grad_gate, grad_up = weight_grads(
        [[(both[e], 0) for e in range(2)], [(both[e], 3) for e in range(2)]], got_rows
    )
    moe = lax.dot_general(hi, returned, TN, preferred_element_type=F32) + lax.dot_general(
        lo, returned, TN, preferred_element_type=F32
    )
    layer_out = (hstate + moe).astype(BF)
    return (layer_out, grad_gate, grad_up, grad_down)


def solution(mesh):
    tok = ("ctx", "exp")
    return jax.shard_map(
        per_device,
        mesh=mesh,
        in_specs=(
            P(tok, None),
            P(tok, "head"),
            P(None, tok, "head"),
            P(None, tok),
            P("head", tok),
            P(),
            P(tok, None),
            P(tok, None),
            P(tok, None, "head"),
            P(tok, None, "head"),
            P(tok, None, "head"),
            P(tok, None),
        ),
        out_specs=(
            P(tok, "head"),
            P(tok, None, "head"),
            P(tok, None, "head"),
            P(tok, None, "head"),
        ),
        check_vma=False,
    )
```

```python
import functools
import math

import jax
import jax.numpy as jnp
from jax import lax
from jax.experimental import pallas as pl
from jax.experimental.pallas import tpu as pltpu
from jax.sharding import PartitionSpec as P


BF = jnp.bfloat16
F32 = jnp.float32
HD = 128
CAP = 10
ROW = 24
RELZ = (-1, 0, 1, -4, -3, -2, 2, 3)
NT = (((1,), (1,)), ((), ()))
TN = (((0,), (0,)), ((), ()))
ANY = pl.BlockSpec(memory_space=pl.ANY)
VM = pl.BlockSpec(memory_space=pltpu.VMEM)


def shift(x, axis, n, d):
    return lax.ppermute(x, axis, [(i, (i + d) % n) for i in range(n)])


def shift_x(x, d):
    return lax.ppermute(x, "ctx", [(i, (i + 2 * d) % 8) for i in range(8)])


def swap_core(x):
    return lax.ppermute(x, "ctx", [(i, i ^ 1) for i in range(8)])


def later(x, *others):
    return lax.optimization_barrier((x, *others))[0]


def near_z(x):
    return jnp.concatenate([shift(x, "exp", 8, 1), x, shift(x, "exp", 8, -1)], 0)


def far_z(three):
    n = three.shape[0] // 3
    far_before = shift(three, "exp", 8, 3)
    far_after = shift(three[: 2 * n], "exp", 8, -3)
    return jnp.concatenate([three, far_before, far_after], 0)


def attention_kernel(last, q_ref, qdoc_ref, *refs):
    pieces = refs[:5]
    if last:
        m_in, l_in, acc_in, o_ref, m_s, l_s, acc, kv, qs, bias, sem = refs[5:]
    else:
        m_s, l_s, acc, kv, qs, bias, sem = refs[5:]
    plan = ((0, 0, 8), (1, 0, 8), (2, 0, 8), (3, 0, 4), (3, 4, 4))
    copies = [
        pltpu.make_async_copy(pieces[p], kv.at[c, pl.ds(lo, n)], sem.at[p])
        for p, (c, lo, n) in enumerate(plan)
    ]
    for cp in copies:
        cp.start()
    ctx = lax.axis_index("ctx")
    z = lax.axis_index("exp")
    me = ctx * 8 + z
    for h in range(8):
        qs[h * 128 : (h + 1) * 128, :] = q_ref[:, h * 128 : (h + 1) * 128]
    if last:
        m_s[...] = m_in[...]
        l_s[...] = l_in[...]
        acc[...] = acc_in[...]
    else:
        m_s[...] = jnp.full(m_s.shape, -1e30, F32)
        l_s[...] = jnp.zeros(l_s.shape, F32)
        acc[...] = jnp.zeros(acc.shape, F32)
    qdoc = qdoc_ref[...].astype(F32)
    first_doc = jnp.min(qdoc)
    row = lax.broadcasted_iota(jnp.int32, (128, 128), 0)
    lane = lax.broadcasted_iota(jnp.int32, (128, 128), 1)
    coef = HD**-0.5 * math.log2(math.e)
    for cp in copies:
        cp.wait()

    def chunk(k, carry):
        dx = jnp.where(k == 1, 3, jnp.where(k == 2, 1, jnp.where(k == 3, 2, 0)))
        kcore = 1 - ctx % 2 if last else ctx % 2
        kctx = ((ctx // 2 + dx) % 4) * 2 + kcore
        docs = kv[k, :, 256:272, :].astype(F32)
        last_doc = jnp.max(docs)

        @pl.when((kctx <= ctx) & (last_doc >= first_doc))
        def _():
            for b, rel in enumerate(RELZ):
                j = kctx * 8 + (z + rel + 8) % 8
                seen = (lane + j * 128 <= row + me * 128) & (
                    docs[b, 0:1, :] == qdoc
                )
                bias[:, b * 128 : (b + 1) * 128] = jnp.where(seen, 0.0, -1e30)

            def group(g, carry2):
                keys = kv[k, :, 0:128, :].reshape(1024, 128)
                vals = kv[k, :, 128:256, :].reshape(1024, 128)
                rows = [pl.ds(pl.multiple_of(g * 512 + i * 256, 256), 256) for i in range(2)]
                raw = [
                    lax.dot_general(qs[r, :], keys, NT, preferred_element_type=F32)
                    for r in rows
                ]
                olds = [m_s[r, :] for r in rows]
                sums = [l_s[r, :] for r in rows]
                accs = [acc[r, :] for r in rows]
                done = []
                for s, old, lsum, a in zip(raw, olds, sums, accs):
                    s = s * coef
                    s = (s.reshape(2, 128, 1024) + bias[...][None]).reshape(256, 1024)
                    new = jnp.maximum(old, jnp.max(s, axis=1, keepdims=True))
                    keep = jnp.exp2(old - new)
                    p = jnp.exp2(s - new[:, 0:1])
                    part = p[:, 0:128]
                    for i in range(1, 8):
                        part = part + p[:, i * 128 : (i + 1) * 128]
                    mixed = lax.dot_general(
                        p.astype(BF),
                        vals,
                        (((1,), (0,)), ((), ())),
                        preferred_element_type=F32,
                    )
                    done.append((new, lsum * keep + part, a * keep + mixed))
                for r, (new, lsum, a) in zip(rows, done):
                    m_s[r, :] = new
                    l_s[r, :] = lsum
                    acc[r, :] = a
                return carry2

            lax.fori_loop(0, 2, group, 0)

        return carry

    lax.fori_loop(0, 4, chunk, 0)
    if last:
        for h in range(8):
            r = slice(h * 128, (h + 1) * 128)
            whole = jnp.sum(l_s[r, :], axis=1, keepdims=True)
            o_ref[:, r] = (acc[r, :] / whole).astype(BF)


def attention(queries, doc_col, pieces, state=()):
    last = bool(state)
    flat = pltpu.VMEM((1024, 128), F32)
    return pl.pallas_call(
        functools.partial(attention_kernel, last),
        out_shape=jax.ShapeDtypeStruct((128, 1024), BF)
        if last
        else [jax.ShapeDtypeStruct((1024, 128), F32)] * 3,
        in_specs=[VM, VM] + [ANY] * 5 + [VM] * len(state),
        out_specs=VM if last else [VM] * 3,
        scratch_shapes=([flat] * 3 if last else [])
        + [
            pltpu.VMEM((4, 8, 272, 128), BF),
            pltpu.VMEM((1024, 128), BF),
            pltpu.VMEM((128, 1024), F32),
            pltpu.SemaphoreType.DMA((5,)),
        ],
        name="attention",
    )(queries, doc_col, *pieces, *state)


def project_kernel(attn_ref, *refs):
    pieces, (o0, o1, o2, o3, ws) = refs[:10], refs[10:]
    ctx = lax.axis_index("ctx")
    z = lax.axis_index("exp")
    me = lax.axis_index("head")
    own = ctx % 2
    plan = ((0, 0, 8), (3, 0, 8), (1, 0, 8), (2, 0, 4), (2, 4, 8))
    for k in range(2):
        core = own if k == 0 else 1 - own
        for p, (dx, lo, hi) in enumerate(plan):
            base = ((ctx // 2 + dx) % 4) * 512 + core * 256
            for i in range(lo, hi):
                at = base + ((z + RELZ[i] + 8) % 8) * 32
                ws[pl.ds(pl.multiple_of(at, 32), 32), :] = pieces[k * 5 + p][
                    (i - lo) * 32 : (i - lo + 1) * 32, :
                ]
    for d, out in enumerate((o0, o1, o2, o3)):
        at = pl.multiple_of(((me + d) % 4) * 512, 512)
        part = lax.dot_general(
            attn_ref[...], ws[pl.ds(at, 512), :], NT, preferred_element_type=F32
        )
        out[...] = part.astype(out.dtype)


def project(attn, pieces):
    return pl.pallas_call(
        project_kernel,
        out_shape=[jax.ShapeDtypeStruct((128, 512), F32)]
        + [jax.ShapeDtypeStruct((128, 512), BF)] * 3,
        in_specs=[VM] * 11,
        out_specs=[VM] * 4,
        scratch_shapes=[pltpu.VMEM((2048, 1024), BF)],
        name="project",
    )(attn, *pieces)


def route_kernel(routes_ref, probs_ref, cot_ref, pick_ref, grad_ref, hi_ref, lo_ref):
    expert = lax.broadcasted_iota(jnp.int32, (128, 128), 0)
    named = jnp.zeros((128, 128), F32)
    weight = jnp.zeros((128, 128), F32)
    for k in range(8):
        hit = routes_ref[k : k + 1, :] == expert
        named = named + jnp.where(hit, 1.0, 0.0)
        weight = weight + jnp.where(hit, probs_ref[k : k + 1, :], 0.0)
    earlier = (
        lax.broadcasted_iota(jnp.int32, (128, 128), 0)
        < lax.broadcasted_iota(jnp.int32, (128, 128), 1)
    )
    rank = jnp.dot(
        named.astype(BF),
        jnp.where(earlier, 1.0, 0.0).astype(BF),
        preferred_element_type=F32,
    )
    place = (named * (rank + 1.0)).astype(BF)
    w1 = weight.astype(BF)
    rest = weight - w1.astype(F32)
    w2 = rest.astype(BF)
    w3 = (rest - w2.astype(F32)).astype(BF)
    size = 384
    for part in range(4):
        r = lax.broadcasted_iota(jnp.int32, (size, 128), 0)
        owner = jnp.zeros((size, 128), jnp.int32)
        for o in range(1, 16):
            owner = owner + jnp.where(r >= o * ROW, 1, 0)
        inner = r - owner * ROW
        second = jnp.where(inner >= CAP, 1, 0)
        slot = inner - second * CAP
        slot = jnp.where(inner >= 2 * CAP, 1000, slot)
        of = (owner + part * 16) * 2 + second
        chosen = jnp.where(
            of == lax.broadcasted_iota(jnp.int32, (size, 128), 1), 1.0, 0.0
        ).astype(BF)
        dot = functools.partial(jnp.dot, preferred_element_type=F32)
        mine = dot(chosen, place) == (slot + 1).astype(F32)
        w = (dot(chosen, w1) + dot(chosen, w2)) + dot(chosen, w3)
        w = jnp.where(mine, w, 0.0)
        pick = jnp.where(mine, 1.0, 0.0).astype(BF)
        at = slice(part * size, (part + 1) * size)
        pick_ref[at, :] = pick
        scale = jnp.sum(w, axis=1, keepdims=True)
        grad_ref[at, :] = (scale * dot(pick, cot_ref[...])).astype(BF)
        hi = w.astype(BF)
        hi_ref[at, :] = hi
        lo_ref[at, :] = (w - hi.astype(F32)).astype(BF)


def route(routes_t, probs_t, cot):
    rows = 64 * ROW
    sq = jax.ShapeDtypeStruct((rows, 128), BF)
    return pl.pallas_call(
        route_kernel,
        out_shape=[sq, jax.ShapeDtypeStruct((rows, 512), BF), sq, sq],
        in_specs=[VM] * 3,
        out_specs=[VM] * 4,
        name="route",
    )(routes_t, probs_t, cot)


def pull(got_ref, e):
    return got_ref[:, e * CAP : (e + 1) * CAP, :].reshape(640, 512)


def share_kernel(ea, eb, got_ref, wa_ref, wb_ref, own, up, down, keep1, keep3, s, x):
    me = lax.axis_index("head")
    step = pl.program_id(0)

    @pl.when(step == 0)
    def _():
        x[...] = pull(got_ref, ea)

    if eb != ea:

        @pl.when(step == 1)
        def _():
            x[...] = pull(got_ref, eb)

    w = jnp.where(step == 0, wa_ref[...], wb_ref[...])
    s[...] = lax.dot_general(x[...], w, NT, preferred_element_type=F32)

    def rows(d, lo, n):
        at = pl.multiple_of(((me + d) % 4) * 160 + lo, 16)
        return s[pl.ds(at, n), :]

    own[...] = rows(0, 0, 160)
    up[0:80, :] = rows(2, 0, 80).astype(BF)
    up[80:160, :] = rows(1, 80, 80).astype(BF)
    down[0:80, :] = rows(2, 80, 80).astype(BF)
    down[80:160, :] = rows(3, 0, 80).astype(BF)
    keep1[...] = rows(1, 0, 80)
    keep3[...] = rows(3, 80, 80)


def share(got, wa, ia, wb, ib):
    shapes = [(160, F32), (160, BF), (160, BF), (80, F32), (80, F32)]
    return pl.pallas_call(
        functools.partial(share_kernel, ia, ib),
        out_shape=[jax.ShapeDtypeStruct((n, 1536), t) for n, t in shapes],
        grid=(2,),
        in_specs=[
            pl.BlockSpec((64, ROW, 512), lambda g: (0, 0, 0)),
            pl.BlockSpec((None, 768, 512), lambda g: (ia, 0, 0)),
            pl.BlockSpec((None, 768, 512), lambda g: (ib, 0, 0)),
        ],
        out_specs=[pl.BlockSpec((n, 768), lambda g: (0, g)) for n, t in shapes],
        scratch_shapes=[pltpu.VMEM((640, 768), F32), pltpu.VMEM((640, 512), BF)],
        name="share",
    )(got, wa, wb)


def add_head(parts):
    own, up, down, keep1, keep3 = parts
    below, above = shift(up, "head", 4, 1), shift(down, "head", 4, -1)
    relay1 = (keep1 + below[:80].astype(F32)).astype(BF)
    relay3 = (keep3 + above[:80].astype(F32)).astype(BF)
    far1, far3 = shift(relay1, "head", 4, 1), shift(relay3, "head", 4, -1)
    return own, below, above, far1, far3


def total(own, below, above, far1, far3, cols):
    lo = (own[0:80, cols] + above[80:160, cols].astype(F32)) + far1[:, cols].astype(F32)
    hi = (own[80:160, cols] + below[80:160, cols].astype(F32)) + far3[:, cols].astype(F32)
    return lo, hi


def active_kernel(e, *refs):
    acts, grad, (hidden, grads) = refs[:5], refs[5:10], refs[10:]
    for c in range(0, 768, 384):
        gates = total(*acts, slice(c, c + 384))
        ups = total(*acts, slice(768 + c, 768 + c + 384))
        back = total(*grad, slice(e * 768 + c, e * 768 + c + 384))
        for i in range(2):
            r = slice(i * 80, (i + 1) * 80)
            sigma = 1.0 / (1.0 + jnp.exp(-gates[i]))
            silu = gates[i] * sigma
            hidden[r, c : c + 384] = (silu * ups[i]).astype(BF)
            gg = back[i] * ups[i] * sigma * (1.0 + gates[i] * (1.0 - sigma))
            grads[r, c : c + 384] = gg.astype(BF)
            grads[r, 768 + c : 768 + c + 384] = (back[i] * silu).astype(BF)


def active(e, acts, grad):
    return pl.pallas_call(
        functools.partial(active_kernel, e),
        out_shape=[
            jax.ShapeDtypeStruct((160, 768), BF),
            jax.ShapeDtypeStruct((160, 1536), BF),
        ],
        in_specs=[VM] * 10,
        out_specs=[VM] * 2,
        name="active",
    )(*acts, *grad)


def gather_head(x):
    below, above = shift(x, "head", 4, 1), shift(x, "head", 4, -1)
    far_a, far_b = shift(below[:80], "head", 4, 1), shift(above[80:], "head", 4, -1)
    return x, below, above, far_a, far_b


def assemble(me, refs, out, cols):
    x, below, above, far_a, far_b = refs
    for d, lo, n, ref in (
        (0, 0, 160, x),
        (3, 0, 160, below),
        (1, 0, 160, above),
        (2, 0, 80, far_a),
        (2, 80, 80, far_b),
    ):
        at = pl.multiple_of(((me + d) % 4) * 160 + lo, 16)
        out[pl.ds(at, n), :] = ref[:, cols]


def down_kernel(*refs):
    w_ref, out, h = refs[10:]
    me = lax.axis_index("head")
    for e in range(2):
        assemble(me, refs[e * 5 : e * 5 + 5], h, slice(0, 768))
        y = jnp.dot(h[...], w_ref[e], preferred_element_type=F32).astype(BF)
        out[:, e * CAP : (e + 1) * CAP, :] = y.reshape(64, CAP, 512)
    out[:, 2 * CAP : ROW, :] = jnp.zeros((64, ROW - 2 * CAP, 512), BF)


def down(hidden, w_down):
    return pl.pallas_call(
        down_kernel,
        out_shape=jax.ShapeDtypeStruct((64, ROW, 512), BF),
        in_specs=[VM] * 11,
        out_specs=VM,
        scratch_shapes=[pltpu.VMEM((640, 768), BF)],
        name="down",
    )(*hidden[0], *hidden[1], w_down)


def weight_grad_kernel(n_out, *refs):
    n = 10 * n_out
    me = lax.axis_index("head")
    first = pl.program_id(0) == 0
    pieces, got, outs, (t, x) = refs[:n], refs[n], refs[n + 1 : -2], refs[-2:]

    for e in range(2):
        now = first if e == 0 else jnp.logical_not(first)

        @pl.when(now & (pl.program_id(1) == 0))
        def _():
            x[...] = pull(got, e)

    for k in range(n_out):
        for e in range(2):

            @pl.when(first if e == 0 else jnp.logical_not(first))
            def _():
                at = (k * 2 + e) * 5
                assemble(me, pieces[at : at + 5], t, slice(0, 256))

        outs[k][...] = lax.dot_general(
            t[...], x[...], TN, preferred_element_type=F32
        ).astype(BF)


def weight_grads(sets, got):
    args, specs = [], []
    for per_expert in sets:
        for e, (pieces, col) in enumerate(per_expert):
            for a in pieces:
                args.append(a)
                specs.append(
                    pl.BlockSpec(
                        (a.shape[0], 256),
                        lambda g, f, col=col, e=e: (0, col + jnp.where(g == e, f, 0)),
                    )
                )
    n_out = len(sets)
    return pl.pallas_call(
        functools.partial(weight_grad_kernel, n_out),
        out_shape=[jax.ShapeDtypeStruct((2, 768, 512), BF)] * n_out,
        grid=(2, 3),
        in_specs=specs + [pl.BlockSpec((64, ROW, 512), lambda g, f: (0, 0, 0))],
        out_specs=[pl.BlockSpec((None, 256, 512), lambda g, f: (g, f, 0))] * n_out,
        scratch_shapes=[pltpu.VMEM((640, 256), BF), pltpu.VMEM((640, 512), BF)],
        name="weight_grads",
    )(*args, got)


def exchange(x):
    return lax.all_to_all(
        x.reshape(64, ROW, 512), ("ctx", "exp"), split_axis=0, concat_axis=0, tiled=True
    )


def per_device(
    resid,
    queries,
    rotated_key_value_pairs,
    doc_ids,
    out_weight,
    norm_gain,
    routes,
    probs,
    w_gate,
    w_up,
    w_down,
    cotangent,
):
    head = lax.axis_index("head")
    packed = jnp.concatenate(
        [
            rotated_key_value_pairs.reshape(256, 128),
            jnp.broadcast_to(doc_ids.astype(BF), (16, 128)),
        ],
        0,
    )
    own_cot = lax.dynamic_slice_in_dim(cotangent, head * 512, 512, 1)
    pick, send_grads, hi, lo = route(routes.T, probs.T, own_cot)
    wthree = near_z(out_weight.T)
    three = later(near_z(packed), pick, wthree)
    z0 = far_z(three).reshape(8, 272, 128)
    below, above = shift_x(z0, 1), shift_x(z0, -1)
    z0_swapped = swap_core(z0)
    w0 = far_z(later(wthree, z0))
    far_a = shift_x(later(below, w0, z0_swapped)[:4], 1)
    far_b = shift_x(later(above, w0, z0_swapped)[4:], -1)
    pieces = (z0, below, above, far_a, far_b)
    doc_col = doc_ids.reshape(128, 1)
    w0 = later(w0, far_a, far_b)
    wbelow = shift_x(w0, 1)
    wabove = shift_x(w0, -1)
    swapped = [z0_swapped]
    for p in pieces[1:]:
        swapped.append(swap_core(p))
    state = attention(queries, doc_col, pieces)
    wfar_a = shift_x(later(wbelow, *state)[:128], 1)
    wfar_b = shift_x(later(wabove, *state)[128:], -1)
    got_grads = exchange(later(send_grads, wbelow, wabove, *state))
    attn = attention(later(queries, wbelow, wabove), doc_col, swapped, state)
    w_pieces = (w0, wbelow, wabove, wfar_a, wfar_b)
    w_pieces = w_pieces + tuple(swap_core(later(p, *state)) for p in w_pieces)
    o0, o1, o2, o3 = project(attn, w_pieces)
    attn_sum = (o0 + shift(o1, "head", 4, 1).astype(F32)) + (
        shift(o2, "head", 4, 2).astype(F32) + shift(o3, "head", 4, -1).astype(F32)
    )
    own_resid = lax.dynamic_slice_in_dim(resid, head * 512, 512, 1)
    hstate = (own_resid.astype(F32) + attn_sum).astype(BF).astype(F32)
    square = jnp.sum(hstate * hstate, axis=-1).reshape(1, 128)
    square = (square + shift(square, "head", 4, 1)) + (
        shift(square, "head", 4, 2) + shift(square, "head", 4, -1)
    )
    inverse = lax.rsqrt(square.reshape(128, 1) / 2048.0 + 1e-06)
    gain = lax.dynamic_slice_in_dim(norm_gain, head * 512, 512, 0)
    normed = (hstate * inverse * gain).astype(BF)

    send_rows = jnp.dot(pick, normed, preferred_element_type=F32).astype(BF)
    got_rows = exchange(send_rows)
    back = add_head(share(later(got_grads, send_rows), w_down, 0, w_down, 1))
    got_rows = later(got_rows, *back[1:])
    terms = [share(got_rows, w_gate, e, w_up, e) for e in range(2)]
    acts = [add_head(terms[e]) for e in range(2)]
    shares = [active(e, acts[e], back) for e in range(2)]
    hidden = [gather_head(shares[e][0]) for e in range(2)]
    returned = exchange(down(hidden, w_down)).reshape(64 * ROW, 512)
    both = [
        gather_head(later(shares[e][1], hidden[1][1], hidden[0][1]))
        for e in range(2)
    ]
    (grad_down,) = weight_grads([[(hidden[e], 0) for e in range(2)]], got_grads)
    grad_gate, grad_up = weight_grads(
        [[(both[e], 0) for e in range(2)], [(both[e], 3) for e in range(2)]], got_rows
    )
    moe = lax.dot_general(hi, returned, TN, preferred_element_type=F32) + lax.dot_general(
        lo, returned, TN, preferred_element_type=F32
    )
    layer_out = (hstate + moe).astype(BF)
    return (layer_out, grad_gate, grad_up, grad_down)


def solution(mesh):
    tok = ("ctx", "exp")
    return jax.shard_map(
        per_device,
        mesh=mesh,
        in_specs=(
            P(tok, None),
            P(tok, "head"),
            P(None, tok, "head"),
            P(None, tok),
            P("head", tok),
            P(),
            P(tok, None),
            P(tok, None),
            P(tok, None, "head"),
            P(tok, None, "head"),
            P(tok, None, "head"),
            P(tok, None),
        ),
        out_specs=(
            P(tok, "head"),
            P(tok, None, "head"),
            P(tok, None, "head"),
            P(tok, None, "head"),
        ),
        check_vma=False,
    )
```

```python
import functools
import math

import jax
import jax.numpy as jnp
from jax import lax
from jax.experimental import pallas as pl
from jax.experimental.pallas import tpu as pltpu
from jax.sharding import PartitionSpec as P


BF = jnp.bfloat16
F32 = jnp.float32
HD = 128
CAP = 10
ROW = 24
RELZ = (-1, 0, 1, -4, -3, -2, 2, 3)
NT = (((1,), (1,)), ((), ()))
TN = (((0,), (0,)), ((), ()))
ANY = pl.BlockSpec(memory_space=pl.ANY)
VM = pl.BlockSpec(memory_space=pltpu.VMEM)


def shift(x, axis, n, d):
    return lax.ppermute(x, axis, [(i, (i + d) % n) for i in range(n)])


def shift_x(x, d):
    return lax.ppermute(x, "ctx", [(i, (i + 2 * d) % 8) for i in range(8)])


def swap_core(x):
    return lax.ppermute(x, "ctx", [(i, i ^ 1) for i in range(8)])


def later(x, *others):
    return lax.optimization_barrier((x, *others))[0]


def near_z(x):
    return jnp.concatenate([shift(x, "exp", 8, 1), x, shift(x, "exp", 8, -1)], 0)


def far_z(three):
    n = three.shape[0] // 3
    far_before = shift(three, "exp", 8, 3)
    far_after = shift(three[: 2 * n], "exp", 8, -3)
    return jnp.concatenate([three, far_before, far_after], 0)


def attention_kernel(last, q_ref, qdoc_ref, *refs):
    pieces = refs[:5]
    if last:
        m_in, l_in, acc_in, o_ref, m_s, l_s, acc, kv, qs, bias, sem = refs[5:]
    else:
        m_s, l_s, acc, kv, qs, bias, sem = refs[5:]
    plan = ((0, 0, 8), (1, 0, 8), (2, 0, 8), (3, 0, 4), (3, 4, 4))
    copies = [
        pltpu.make_async_copy(pieces[p], kv.at[c, pl.ds(lo, n)], sem.at[p])
        for p, (c, lo, n) in enumerate(plan)
    ]
    for cp in copies:
        cp.start()
    ctx = lax.axis_index("ctx")
    z = lax.axis_index("exp")
    me = ctx * 8 + z
    for h in range(8):
        qs[h * 128 : (h + 1) * 128, :] = q_ref[:, h * 128 : (h + 1) * 128]
    if last:
        m_s[...] = m_in[...]
        l_s[...] = l_in[...]
        acc[...] = acc_in[...]
    else:
        m_s[...] = jnp.full(m_s.shape, -1e30, F32)
        l_s[...] = jnp.zeros(l_s.shape, F32)
        acc[...] = jnp.zeros(acc.shape, F32)
    qdoc = qdoc_ref[...].astype(F32)
    first_doc = jnp.min(qdoc)
    row = lax.broadcasted_iota(jnp.int32, (128, 128), 0)
    lane = lax.broadcasted_iota(jnp.int32, (128, 128), 1)
    coef = HD**-0.5 * math.log2(math.e)
    for cp in copies:
        cp.wait()

    def chunk(k, carry):
        dx = jnp.where(k == 1, 3, jnp.where(k == 2, 1, jnp.where(k == 3, 2, 0)))
        kcore = 1 - ctx % 2 if last else ctx % 2
        kctx = ((ctx // 2 + dx) % 4) * 2 + kcore
        docs = kv[k, :, 256:272, :].astype(F32)
        last_doc = jnp.max(docs)

        @pl.when((kctx <= ctx) & (last_doc >= first_doc))
        def _():
            for b, rel in enumerate(RELZ):
                j = kctx * 8 + (z + rel + 8) % 8
                seen = (lane + j * 128 <= row + me * 128) & (
                    docs[b, 0:1, :] == qdoc
                )
                bias[:, b * 128 : (b + 1) * 128] = jnp.where(seen, 0.0, -1e30)

            def group(g, carry2):
                keys = kv[k, :, 0:128, :].reshape(1024, 128)
                vals = kv[k, :, 128:256, :].reshape(1024, 128)
                rows = [pl.ds(pl.multiple_of(g * 512 + i * 256, 256), 256) for i in range(2)]
                raw = [
                    lax.dot_general(qs[r, :], keys, NT, preferred_element_type=F32)
                    for r in rows
                ]
                olds = [m_s[r, :] for r in rows]
                sums = [l_s[r, :] for r in rows]
                accs = [acc[r, :] for r in rows]
                done = []
                for s, old, lsum, a in zip(raw, olds, sums, accs):
                    s = s * coef
                    s = (s.reshape(2, 128, 1024) + bias[...][None]).reshape(256, 1024)
                    new = jnp.maximum(old, jnp.max(s, axis=1, keepdims=True))
                    keep = jnp.exp2(old - new)
                    p = jnp.exp2(s - new[:, 0:1])
                    part = p[:, 0:128]
                    for i in range(1, 8):
                        part = part + p[:, i * 128 : (i + 1) * 128]
                    mixed = lax.dot_general(
                        p.astype(BF),
                        vals,
                        (((1,), (0,)), ((), ())),
                        preferred_element_type=F32,
                    )
                    done.append((new, lsum * keep + part, a * keep + mixed))
                for r, (new, lsum, a) in zip(rows, done):
                    m_s[r, :] = new
                    l_s[r, :] = lsum
                    acc[r, :] = a
                return carry2

            lax.fori_loop(0, 2, group, 0)

        return carry

    lax.fori_loop(0, 4, chunk, 0)
    if last:
        for h in range(8):
            r = slice(h * 128, (h + 1) * 128)
            whole = jnp.sum(l_s[r, :], axis=1, keepdims=True)
            o_ref[:, r] = (acc[r, :] / whole).astype(BF)


def attention(queries, doc_col, pieces, state=()):
    last = bool(state)
    flat = pltpu.VMEM((1024, 128), F32)
    return pl.pallas_call(
        functools.partial(attention_kernel, last),
        out_shape=jax.ShapeDtypeStruct((128, 1024), BF)
        if last
        else [jax.ShapeDtypeStruct((1024, 128), F32)] * 3,
        in_specs=[VM, VM] + [ANY] * 5 + [VM] * len(state),
        out_specs=VM if last else [VM] * 3,
        scratch_shapes=([flat] * 3 if last else [])
        + [
            pltpu.VMEM((4, 8, 272, 128), BF),
            pltpu.VMEM((1024, 128), BF),
            pltpu.VMEM((128, 1024), F32),
            pltpu.SemaphoreType.DMA((5,)),
        ],
        name="attention",
    )(queries, doc_col, *pieces, *state)


def project_kernel(attn_ref, *refs):
    pieces, (o0, o1, o2, o3, ws) = refs[:10], refs[10:]
    ctx = lax.axis_index("ctx")
    z = lax.axis_index("exp")
    me = lax.axis_index("head")
    own = ctx % 2
    plan = ((0, 0, 8), (3, 0, 8), (1, 0, 8), (2, 0, 4), (2, 4, 8))
    for k in range(2):
        core = own if k == 0 else 1 - own
        for p, (dx, lo, hi) in enumerate(plan):
            base = ((ctx // 2 + dx) % 4) * 512 + core * 256
            for i in range(lo, hi):
                at = base + ((z + RELZ[i] + 8) % 8) * 32
                ws[pl.ds(pl.multiple_of(at, 32), 32), :] = pieces[k * 5 + p][
                    (i - lo) * 32 : (i - lo + 1) * 32, :
                ]
    for d, out in enumerate((o0, o1, o2, o3)):
        at = pl.multiple_of(((me + d) % 4) * 512, 512)
        part = lax.dot_general(
            attn_ref[...], ws[pl.ds(at, 512), :], NT, preferred_element_type=F32
        )
        out[...] = part.astype(out.dtype)


def project(attn, pieces):
    return pl.pallas_call(
        project_kernel,
        out_shape=[jax.ShapeDtypeStruct((128, 512), F32)]
        + [jax.ShapeDtypeStruct((128, 512), BF)] * 3,
        in_specs=[VM] * 11,
        out_specs=[VM] * 4,
        scratch_shapes=[pltpu.VMEM((2048, 1024), BF)],
        name="project",
    )(attn, *pieces)


def route_kernel(routes_ref, probs_ref, cot_ref, pick_ref, grad_ref, hi_ref, lo_ref):
    expert = lax.broadcasted_iota(jnp.int32, (128, 128), 0)
    named = jnp.zeros((128, 128), F32)
    weight = jnp.zeros((128, 128), F32)
    for k in range(8):
        hit = routes_ref[k : k + 1, :] == expert
        named = named + jnp.where(hit, 1.0, 0.0)
        weight = weight + jnp.where(hit, probs_ref[k : k + 1, :], 0.0)
    earlier = (
        lax.broadcasted_iota(jnp.int32, (128, 128), 0)
        < lax.broadcasted_iota(jnp.int32, (128, 128), 1)
    )
    rank = jnp.dot(
        named.astype(BF),
        jnp.where(earlier, 1.0, 0.0).astype(BF),
        preferred_element_type=F32,
    )
    place = (named * (rank + 1.0)).astype(BF)
    w1 = weight.astype(BF)
    rest = weight - w1.astype(F32)
    w2 = rest.astype(BF)
    w3 = (rest - w2.astype(F32)).astype(BF)
    size = 384
    for part in range(4):
        r = lax.broadcasted_iota(jnp.int32, (size, 128), 0)
        owner = jnp.zeros((size, 128), jnp.int32)
        for o in range(1, 16):
            owner = owner + jnp.where(r >= o * ROW, 1, 0)
        inner = r - owner * ROW
        second = jnp.where(inner >= CAP, 1, 0)
        slot = inner - second * CAP
        slot = jnp.where(inner >= 2 * CAP, 1000, slot)
        of = (owner + part * 16) * 2 + second
        chosen = jnp.where(
            of == lax.broadcasted_iota(jnp.int32, (size, 128), 1), 1.0, 0.0
        ).astype(BF)
        dot = functools.partial(jnp.dot, preferred_element_type=F32)
        mine = dot(chosen, place) == (slot + 1).astype(F32)
        w = (dot(chosen, w1) + dot(chosen, w2)) + dot(chosen, w3)
        w = jnp.where(mine, w, 0.0)
        pick = jnp.where(mine, 1.0, 0.0).astype(BF)
        at = slice(part * size, (part + 1) * size)
        pick_ref[at, :] = pick
        scale = jnp.sum(w, axis=1, keepdims=True)
        grad_ref[at, :] = (scale * dot(pick, cot_ref[...])).astype(BF)
        hi = w.astype(BF)
        hi_ref[at, :] = hi
        lo_ref[at, :] = (w - hi.astype(F32)).astype(BF)


def route(routes_t, probs_t, cot):
    rows = 64 * ROW
    sq = jax.ShapeDtypeStruct((rows, 128), BF)
    return pl.pallas_call(
        route_kernel,
        out_shape=[sq, jax.ShapeDtypeStruct((rows, 512), BF), sq, sq],
        in_specs=[VM] * 3,
        out_specs=[VM] * 4,
        name="route",
    )(routes_t, probs_t, cot)


def pull(got_ref, e):
    return got_ref[:, e * CAP : (e + 1) * CAP, :].reshape(640, 512)


def share_kernel(ea, eb, norm, got_ref, wa_ref, wb_ref, *refs):
    if norm:
        gain_ref, own, up, down, keep1, keep3, s, x, q = refs
    else:
        own, up, down, keep1, keep3, s, x = refs
    me = lax.axis_index("head")
    step = pl.program_id(0)

    @pl.when(step == 0)
    def _():
        if norm:
            h = pull(got_ref, ea).astype(F32)
            x[...] = (h * gain_ref[...]).astype(BF)
            q[...] = jnp.broadcast_to(jnp.sum(h * h, axis=1, keepdims=True), (640, 128))
        else:
            x[...] = pull(got_ref, ea)

    if eb != ea:

        @pl.when(step == 1)
        def _():
            x[...] = pull(got_ref, eb)

    w = jnp.where(step == 0, wa_ref[...], wb_ref[...])
    s[:, 0:768] = lax.dot_general(x[...], w, NT, preferred_element_type=F32)
    if norm:
        s[:, 768:896] = q[...]

    def rows(d, lo, n):
        at = pl.multiple_of(((me + d) % 4) * 160 + lo, 16)
        return s[pl.ds(at, n), :]

    own[...] = rows(0, 0, 160)
    up[0:80, :] = rows(2, 0, 80).astype(BF)
    up[80:160, :] = rows(1, 80, 80).astype(BF)
    down[0:80, :] = rows(2, 80, 80).astype(BF)
    down[80:160, :] = rows(3, 0, 80).astype(BF)
    keep1[...] = rows(1, 0, 80)
    keep3[...] = rows(3, 80, 80)


def share(got, wa, ia, wb, ib, gain=None):
    norm = gain is not None
    width = 896 if norm else 768
    shapes = [(160, F32), (160, BF), (160, BF), (80, F32), (80, F32)]
    scratch = [pltpu.VMEM((640, width), F32), pltpu.VMEM((640, 512), BF)]
    return pl.pallas_call(
        functools.partial(share_kernel, ia, ib, norm),
        out_shape=[jax.ShapeDtypeStruct((n, 2 * width), t) for n, t in shapes],
        grid=(2,),
        in_specs=[
            pl.BlockSpec((64, ROW, 512), lambda g: (0, 0, 0)),
            pl.BlockSpec((None, 768, 512), lambda g: (ia, 0, 0)),
            pl.BlockSpec((None, 768, 512), lambda g: (ib, 0, 0)),
        ]
        + ([pl.BlockSpec((1, 512), lambda g: (0, 0))] if norm else []),
        out_specs=[pl.BlockSpec((n, width), lambda g: (0, g)) for n, t in shapes],
        scratch_shapes=scratch + ([pltpu.VMEM((640, 128), F32)] if norm else []),
        name="share",
    )(got, wa, wb, *([gain] if norm else []))


def add_head(parts):
    own, up, down, keep1, keep3 = parts
    below, above = shift(up, "head", 4, 1), shift(down, "head", 4, -1)
    relay1 = (keep1 + below[:80].astype(F32)).astype(BF)
    relay3 = (keep3 + above[:80].astype(F32)).astype(BF)
    far1, far3 = shift(relay1, "head", 4, 1), shift(relay3, "head", 4, -1)
    return own, below, above, far1, far3


def total(own, below, above, far1, far3, cols):
    lo = (own[0:80, cols] + above[80:160, cols].astype(F32)) + far1[:, cols].astype(F32)
    hi = (own[80:160, cols] + below[80:160, cols].astype(F32)) + far3[:, cols].astype(F32)
    return lo, hi


def active_kernel(e, *refs):
    acts, grad, (hidden, grads) = refs[:5], refs[5:10], refs[10:]
    squares = total(*acts, slice(768, 896))
    norms = [lax.rsqrt(v[:, 0:1] / 2048.0 + 1e-06) for v in squares]
    for c in range(0, 768, 384):
        gates = total(*acts, slice(c, c + 384))
        ups = total(*acts, slice(896 + c, 896 + c + 384))
        back = total(*grad, slice(e * 768 + c, e * 768 + c + 384))
        for i in range(2):
            r = slice(i * 80, (i + 1) * 80)
            gate, up = gates[i] * norms[i], ups[i] * norms[i]
            sigma = 1.0 / (1.0 + jnp.exp(-gate))
            silu = gate * sigma
            hidden[r, c : c + 384] = (silu * up).astype(BF)
            scaled = back[i] * norms[i]
            gg = scaled * up * sigma * (1.0 + gate * (1.0 - sigma))
            grads[r, c : c + 384] = gg.astype(BF)
            grads[r, 768 + c : 768 + c + 384] = (scaled * silu).astype(BF)


def active(e, acts, grad):
    return pl.pallas_call(
        functools.partial(active_kernel, e),
        out_shape=[
            jax.ShapeDtypeStruct((160, 768), BF),
            jax.ShapeDtypeStruct((160, 1536), BF),
        ],
        in_specs=[VM] * 10,
        out_specs=[VM] * 2,
        name="active",
    )(*acts, *grad)


def gather_head(x):
    below, above = shift(x, "head", 4, 1), shift(x, "head", 4, -1)
    far_a, far_b = shift(below[:80], "head", 4, 1), shift(above[80:], "head", 4, -1)
    return x, below, above, far_a, far_b


def assemble(me, refs, out, cols):
    x, below, above, far_a, far_b = refs
    for d, lo, n, ref in (
        (0, 0, 160, x),
        (3, 0, 160, below),
        (1, 0, 160, above),
        (2, 0, 80, far_a),
        (2, 80, 80, far_b),
    ):
        at = pl.multiple_of(((me + d) % 4) * 160 + lo, 16)
        out[pl.ds(at, n), :] = ref[:, cols]


def down_kernel(*refs):
    w_ref, out, h = refs[10:]
    me = lax.axis_index("head")
    for e in range(2):
        assemble(me, refs[e * 5 : e * 5 + 5], h, slice(0, 768))
        y = jnp.dot(h[...], w_ref[e], preferred_element_type=F32).astype(BF)
        out[:, e * CAP : (e + 1) * CAP, :] = y.reshape(64, CAP, 512)
    out[:, 2 * CAP : ROW, :] = jnp.zeros((64, ROW - 2 * CAP, 512), BF)


def down(hidden, w_down):
    return pl.pallas_call(
        down_kernel,
        out_shape=jax.ShapeDtypeStruct((64, ROW, 512), BF),
        in_specs=[VM] * 11,
        out_specs=VM,
        scratch_shapes=[pltpu.VMEM((640, 768), BF)],
        name="down",
    )(*hidden[0], *hidden[1], w_down)


def weight_grad_kernel(n_out, norm, *refs):
    n = 10 * n_out
    me = lax.axis_index("head")
    first = pl.program_id(0) == 0
    pieces, got, outs, (t, x) = refs[:n], refs[n], refs[n + 1 + norm : -2], refs[-2:]

    for e in range(2):
        now = first if e == 0 else jnp.logical_not(first)

        @pl.when(now & (pl.program_id(1) == 0))
        def _():
            if norm:
                x[...] = (pull(got, e).astype(F32) * refs[n + 1][...]).astype(BF)
            else:
                x[...] = pull(got, e)

    for k in range(n_out):
        for e in range(2):

            @pl.when(first if e == 0 else jnp.logical_not(first))
            def _():
                at = (k * 2 + e) * 5
                assemble(me, pieces[at : at + 5], t, slice(0, 256))

        outs[k][...] = lax.dot_general(
            t[...], x[...], TN, preferred_element_type=F32
        ).astype(BF)


def weight_grads(sets, got, gain=None):
    args, specs = [], []
    for per_expert in sets:
        for e, (pieces, col) in enumerate(per_expert):
            for a in pieces:
                args.append(a)
                specs.append(
                    pl.BlockSpec(
                        (a.shape[0], 256),
                        lambda g, f, col=col, e=e: (0, col + jnp.where(g == e, f, 0)),
                    )
                )
    n_out = len(sets)
    return pl.pallas_call(
        functools.partial(weight_grad_kernel, n_out, int(gain is not None)),
        out_shape=[jax.ShapeDtypeStruct((2, 768, 512), BF)] * n_out,
        grid=(2, 3),
        in_specs=specs
        + [pl.BlockSpec((64, ROW, 512), lambda g, f: (0, 0, 0))]
        + ([] if gain is None else [pl.BlockSpec((1, 512), lambda g, f: (0, 0))]),
        out_specs=[pl.BlockSpec((None, 256, 512), lambda g, f: (g, f, 0))] * n_out,
        scratch_shapes=[pltpu.VMEM((640, 256), BF), pltpu.VMEM((640, 512), BF)],
        name="weight_grads",
    )(*args, got, *([] if gain is None else [gain]))


def exchange(x):
    return lax.all_to_all(
        x.reshape(64, ROW, 512), ("ctx", "exp"), split_axis=0, concat_axis=0, tiled=True
    )


def per_device(
    resid,
    queries,
    rotated_key_value_pairs,
    doc_ids,
    out_weight,
    norm_gain,
    routes,
    probs,
    w_gate,
    w_up,
    w_down,
    cotangent,
):
    head = lax.axis_index("head")
    packed = jnp.concatenate(
        [
            rotated_key_value_pairs.reshape(256, 128),
            jnp.broadcast_to(doc_ids.astype(BF), (16, 128)),
        ],
        0,
    )
    own_cot = lax.dynamic_slice_in_dim(cotangent, head * 512, 512, 1)
    pick, send_grads, hi, lo = route(routes.T, probs.T, own_cot)
    wthree = near_z(out_weight.T)
    three = later(near_z(packed), pick, wthree)
    z0 = far_z(three).reshape(8, 272, 128)
    below, above = shift_x(z0, 1), shift_x(z0, -1)
    z0_swapped = swap_core(z0)
    w0 = far_z(later(wthree, z0))
    far_a = shift_x(later(below, w0, z0_swapped)[:4], 1)
    far_b = shift_x(later(above, w0, z0_swapped)[4:], -1)
    pieces = (z0, below, above, far_a, far_b)
    doc_col = doc_ids.reshape(128, 1)
    w0 = later(w0, far_a, far_b)
    wbelow = shift_x(w0, 1)
    wabove = shift_x(w0, -1)
    swapped = [z0_swapped]
    for p in pieces[1:]:
        swapped.append(swap_core(p))
    state = attention(queries, doc_col, pieces)
    wfar_a = shift_x(later(wbelow, *state)[:128], 1)
    wfar_b = shift_x(later(wabove, *state)[128:], -1)
    got_grads = exchange(later(send_grads, wbelow, wabove, *state))
    attn = attention(later(queries, wbelow, wabove), doc_col, swapped, state)
    w_pieces = (w0, wbelow, wabove, wfar_a, wfar_b)
    w_pieces = w_pieces + tuple(swap_core(later(p, *state)) for p in w_pieces)
    o0, o1, o2, o3 = project(attn, w_pieces)
    attn_sum = (o0 + shift(o1, "head", 4, 1).astype(F32)) + (
        shift(o2, "head", 4, 2).astype(F32) + shift(o3, "head", 4, -1).astype(F32)
    )
    own_resid = lax.dynamic_slice_in_dim(resid, head * 512, 512, 1)
    hstate = (own_resid.astype(F32) + attn_sum).astype(BF).astype(F32)
    gain = lax.dynamic_slice_in_dim(norm_gain, head * 512, 512, 0).reshape(1, 512)
    send_rows = jnp.dot(pick, hstate.astype(BF), preferred_element_type=F32).astype(BF)
    got_rows = exchange(send_rows)
    back = add_head(share(later(got_grads, send_rows), w_down, 0, w_down, 1))
    got_rows = later(got_rows, *back[1:])
    terms = [share(got_rows, w_gate, e, w_up, e, gain) for e in range(2)]
    acts = [add_head(terms[e]) for e in range(2)]
    shares = [active(e, acts[e], back) for e in range(2)]
    hidden = [gather_head(shares[e][0]) for e in range(2)]
    returned = exchange(down(hidden, w_down)).reshape(64 * ROW, 512)
    both = [
        gather_head(later(shares[e][1], hidden[1][1], hidden[0][1]))
        for e in range(2)
    ]
    (grad_down,) = weight_grads([[(hidden[e], 0) for e in range(2)]], got_grads)
    grad_gate, grad_up = weight_grads(
        [[(both[e], 0) for e in range(2)], [(both[e], 3) for e in range(2)]], got_rows, gain
    )
    moe = lax.dot_general(hi, returned, TN, preferred_element_type=F32) + lax.dot_general(
        lo, returned, TN, preferred_element_type=F32
    )
    layer_out = (hstate + moe).astype(BF)
    return (layer_out, grad_gate, grad_up, grad_down)


def solution(mesh):
    tok = ("ctx", "exp")
    return jax.shard_map(
        per_device,
        mesh=mesh,
        in_specs=(
            P(tok, None),
            P(tok, "head"),
            P(None, tok, "head"),
            P(None, tok),
            P("head", tok),
            P(),
            P(tok, None),
            P(tok, None),
            P(tok, None, "head"),
            P(tok, None, "head"),
            P(tok, None, "head"),
            P(tok, None),
        ),
        out_specs=(
            P(tok, "head"),
            P(tok, None, "head"),
            P(tok, None, "head"),
            P(tok, None, "head"),
        ),
        check_vma=False,
    )
```
